512 devices in a mesh: src: 4 (over y), seq: 8 (over z_hi, core), head: 16 (over z_lo, x).
Axes of the slice: x: 4, y: 4, z: 16 (z_hi: 4, z_lo: 4; z = z_hi * 4 + z_lo), core: 2. Of those that a mesh axis runs over, the one named last changes fastest.
Arguments:
- enc_out: bfloat16 [32768, 4096], P(('src', 'seq'), 'head'), parts along dimension 0, may hold values from -9 to 9
- enc_gain: float32 [4096], replicated, may hold values from 0.25 to 1.75
- key_weight: bfloat16 [4096, 4096], P('seq', 'head'), may hold values from -1 to 1
- value_weight: bfloat16 [4096, 4096], P('seq', 'head'), may hold values from -0.09375 to 0.09375
- query_weight: bfloat16 [4096, 4096], P('seq', 'head'), may hold values from -2 to 2
- out_weight: bfloat16 [4096, 4096], P('head', 'seq'), may hold values from -0.09375 to 0.09375
- dec_gain: float32 [4096], replicated, may hold values from 0.25 to 1.75
- beam_state: float32 [64, 4096], P('src'), parts along dimension 0, may hold values from -7 to 7
- parents: int32 [8, 16], P('src'), parts along dimension 0, may hold values from 0 to 15
- token_embed: bfloat16 [8, 16, 4096], P('src'), parts along dimension 0, may hold values from -6 to 6
Outputs:
- final_state: float32 [64, 4096], P('src'), parts along dimension 0
- attended: float32 [64, 4096], P('src'), parts along dimension 0
The draws below stay inside these ranges and needn't reach their ends.
There are 4 independent parts, one for each index of `src`. The reference program is written for one: setup_inputs(seed, part) draws one part's arguments, and reference() takes and returns one part's arrays. A program takes and returns all parts, laid end to end along the dimension named above; an argument that names none is the same for every part. Nothing has to cross between parts.
All inputs are finite; a program needn't handle non-finite values.
Results may differ from the reference program's by a relative error of at most 0.013.
The reference program's roundings to bfloat16 on the way (of `memory`, `normed`, `query`, `weights` and `context`) count: a program that leaves them out, or rounds other values in their place, can miss the bound.
Values may be sent and summed in bfloat16 or wider, within the bound.
A program may use at most 64 MiB of HBM per device.

```python
import jax
import jax.numpy as jnp
from jax import lax

D = 4096
HEADS = 64
HEAD_DIM = 64
BEAMS = 16
STEPS = 2
SRC_LEN = 8192


def shared_direction():
    index = jnp.arange(D, dtype=jnp.float32)
    return 1.4142135 * jnp.cos(2.3999632 * index)


def head_pattern(key):
    order = jax.random.permutation(jax.random.fold_in(key, 7001), HEADS)
    chosen = (order < HEADS // 4).astype(jnp.float32)
    signs = jax.random.randint(jax.random.fold_in(key, 7002), (HEADS, HEAD_DIM), 0, 2).astype(jnp.float32) * 2.0 - 1.0
    return (signs * chosen[:, None]).reshape(D)


def base_noise(key, shape):
    return jnp.clip(jax.random.normal(key, shape, jnp.float32), -4.0, 4.0)


def drawn_weight(key, salt, noise_scale):
    amplify = 64.0 * HEAD_DIM ** (-0.5)
    noise = base_noise(jax.random.fold_in(key, salt), (D, D)) * (noise_scale * D ** (-0.5))
    pattern = head_pattern(key)
    return noise + amplify / D * shared_direction()[:, None] * pattern[None, :]


def draw_key_weight(key, part):
    return drawn_weight(key, 8101, 1.0).astype(jnp.bfloat16)


def draw_query_weight(key, part):
    return drawn_weight(key, 8102, 3.0).astype(jnp.bfloat16)


def draw_enc_out(key, part):
    noise = base_noise(jax.random.fold_in(key, 8201), (SRC_LEN, D))
    amount = jnp.clip(jax.random.normal(jax.random.fold_in(key, 8203), (SRC_LEN, 1), jnp.float32), -3.5, 3.5)
    return (noise + amount * shared_direction()[None, :]).astype(jnp.bfloat16)


def draw_beam_state(key, part):
    noise = base_noise(jax.random.fold_in(key, 8301), (BEAMS, D))
    amount = jax.random.uniform(jax.random.fold_in(key, 8303), (BEAMS, 1), jnp.float32, -1.5, 1.5)
    return noise + amount * shared_direction()[None, :]


def draw_token_embed(key, part):
    noise = base_noise(jax.random.fold_in(key, 8401), (STEPS, BEAMS, D))
    amount = jax.random.uniform(jax.random.fold_in(key, 8402), (STEPS, BEAMS, 1), jnp.float32, -1.0, 1.0)
    return (noise + amount * shared_direction()[None, None, :]).astype(jnp.bfloat16)


def plant(values, own_key, smallest, high):
    longest = values.shape.index(max(values.shape))
    spots = []
    for shift in (0, 1):
        where = [jax.random.randint(jax.random.fold_in(own_key, axis), (), 0, length) for axis, length in enumerate(values.shape)]
        where[longest] = (where[longest] + shift) % values.shape[longest]
        spots.append(tuple(where))
    return values.at[spots[0]].set(smallest).at[spots[1]].set(high)


def level_of(key, dims, split, least, largest):
    loudness = 1.0
    for position, shards_of in split:
        draws = jax.random.uniform(jax.random.fold_in(jax.random.fold_in(key, 6), position), (shards_of,), jnp.float32, least / len(split), largest / len(split))
        loudness = loudness * jnp.repeat(jnp.exp(draws), dims[position] // shards_of).reshape((-1,) + (1,) * (len(dims) - 1 - position))
    return loudness


def bell_draw(own_key, dims, scale, bound, shards=(), kind=jnp.bfloat16):
    loudness = level_of(own_key, dims, shards, -0.22, 0.18) if shards else 1.0
    entries = jax.random.normal(own_key, dims, jnp.float32) * scale * loudness
    return jnp.minimum(jnp.maximum(entries, -bound), bound).astype(kind)


def setup_inputs(seed: int = 0, part: int = 0) -> dict:
    arg_keys = jax.random.split(jax.random.key(seed), 11)
    part_keys = jax.random.split(jax.random.fold_in(arg_keys[10], part), 11)
    return {
        "enc_out": draw_enc_out(jax.random.fold_in(jax.random.fold_in(arg_keys[10], part), 71), part),
        "enc_gain": jnp.clip(1.0 + 0.15 * jax.random.normal(arg_keys[1], (D,), jnp.float32), 0.25, 1.75),
        "key_weight": draw_key_weight(jax.random.fold_in(arg_keys[10], 71), part),
        "value_weight": bell_draw(arg_keys[3], (D, D), D ** -0.5, 0.09375, ((0, 8), (1, 16))),
        "query_weight": draw_query_weight(jax.random.fold_in(arg_keys[10], 71), part),
        "out_weight": bell_draw(arg_keys[5], (D, D), D ** -0.5, 0.09375, ((0, 16), (1, 8))),
        "dec_gain": jnp.clip(1.0 + 0.15 * jax.random.normal(arg_keys[6], (D,), jnp.float32), 0.25, 1.75),
        "beam_state": draw_beam_state(jax.random.fold_in(jax.random.fold_in(arg_keys[10], part), 71), part),
        "parents": plant(jax.random.randint(part_keys[8], (STEPS, BEAMS), 0, BEAMS), jax.random.fold_in(part_keys[8], 1), 0, BEAMS - 1).astype(jnp.int32),
        "token_embed": draw_token_embed(jax.random.fold_in(jax.random.fold_in(arg_keys[10], part), 71), part),
    }


def rms_norm(values, gain):
    mean_square = lax.optimization_barrier(jnp.mean(values * values, axis=-1, keepdims=True))
    return values * jax.lax.rsqrt(mean_square + 1e-06) * gain

def reference(enc_out, enc_gain, key_weight, value_weight, query_weight, out_weight, dec_gain, beam_state, parents, token_embed):
    memory = rms_norm(enc_out.astype(jnp.float32), enc_gain).astype(jnp.bfloat16)
    keys = jnp.dot(memory, key_weight, preferred_element_type=jnp.float32).astype(jnp.bfloat16)
    values = jnp.dot(memory, value_weight, preferred_element_type=jnp.float32).astype(jnp.bfloat16)
    keys = keys.reshape(SRC_LEN, HEADS, HEAD_DIM).astype(jnp.float32)
    values = values.reshape(SRC_LEN, HEADS, HEAD_DIM).astype(jnp.float32)
    state = beam_state
    attended = jnp.zeros((BEAMS, D), jnp.float32)
    for step in range(STEPS):
        state = state[parents[step]] + token_embed[step].astype(jnp.float32)
        normed = rms_norm(state, dec_gain).astype(jnp.bfloat16)
        query = jnp.dot(normed, query_weight, preferred_element_type=jnp.float32).astype(jnp.bfloat16)
        query = query.reshape(BEAMS, HEADS, HEAD_DIM).astype(jnp.float32)
        scores = jnp.einsum('bhd,shd->bhs', query, keys) * 0.125
        top = lax.optimization_barrier(jnp.max(scores, axis=-1, keepdims=True))
        expo = jnp.exp(scores - top)
        total = lax.optimization_barrier(jnp.sum(expo, axis=-1))
        weights = expo.astype(jnp.bfloat16).astype(jnp.float32)
        context = jnp.einsum('bhs,shd->bhd', weights, values) / total[..., None]
        context = context.astype(jnp.bfloat16).reshape(BEAMS, D)
        projected = jnp.dot(context, out_weight, preferred_element_type=jnp.float32)
        state = state + projected
        attended = attended + projected
    return (state, attended)
```

```python
import functools

import jax
import jax.numpy as jnp
from jax import lax
from jax.experimental import pallas as pl
from jax.experimental.pallas import tpu as pltpu
from jax.sharding import PartitionSpec as P

MESH = pl.DeviceIdType.MESH
HEAD_DIM = 64
BEAMS = 16
STEPS = 2
SEQ = 8
HEAD = 16


def rms_norm(values, gain):
    mean_square = jnp.mean(values * values, axis=-1, keepdims=True)
    return values * lax.rsqrt(mean_square + 1e-06) * gain


def decode_kernel(
    keys, vals, wq, wo, gain, first, parents, tokens,
    out_state, out_att,
    state, nrm, q_own, q_all, c_own, c_all, t_own, t_all, p_own, p_all, f_own, f_all, g_all,
    q_ss, q_rs, c_ss, c_rs, t_ss, t_rs, p_ss, p_rs, f_ss, f_rs, g_ss, g_rs,
):
    s = lax.axis_index("seq")
    c = lax.axis_index("head")
    seq_peers = [lax.rem(s + k, SEQ) for k in range(1, SEQ)]
    head_peers = [lax.rem(c + k, HEAD) for k in range(1, HEAD)]

    barrier = pltpu.get_barrier_semaphore()
    for p in seq_peers:
        pl.semaphore_signal(barrier, inc=1, device_id={"seq": p}, device_id_type=MESH)
    for p in head_peers:
        pl.semaphore_signal(barrier, inc=1, device_id={"head": p}, device_id_type=MESH)
    pl.semaphore_wait(barrier, SEQ + HEAD - 2)

    sent = []

    def send(src, dst, ss, rs, where):
        copy = pltpu.make_async_remote_copy(
            src_ref=src, dst_ref=dst, send_sem=ss, recv_sem=rs,
            device_id=where, device_id_type=MESH,
        )
        copy.start()
        sent.append(copy)

    def arrived(dst, rs, ss, where):
        pltpu.make_async_remote_copy(
            src_ref=dst, dst_ref=dst, send_sem=ss, recv_sem=rs,
            device_id=where, device_id_type=MESH,
        ).wait_recv()

    col_head = lax.broadcasted_iota(jnp.int32, (BEAMS, 256), 1) // HEAD_DIM
    lane = lax.broadcasted_iota(jnp.int32, (8, 128), 1)

    for t in range(STEPS):
        for b in range(BEAMS):
            source = first[parents[t, b]] if t == 0 else state[t - 1, parents[t, b]]
            row = source + tokens[t, b]
            square = jnp.sum(jnp.sum(row * row, axis=0), axis=(0, 1), keepdims=True) * (1.0 / 4096.0)
            state[t, b] = row
            nrm[b] = row * lax.rsqrt(square + 1e-06)[None] * gain[...]
        part = jnp.zeros((BEAMS, 256), jnp.float32)
        for j in range(4):
            part += jnp.dot(
                nrm[:, s, j, :].astype(jnp.bfloat16), wq[pl.ds(128 * j, 128), :],
                preferred_element_type=jnp.float32,
            )
        q_own[t] = part
        q_all[t, s] = part
        for k, p in enumerate(seq_peers):
            send(q_own.at[t], q_all.at[t, s], q_ss.at[t, k], q_rs.at[t, s], {"seq": p})
        for k, p in enumerate(seq_peers):
            arrived(q_all.at[t, p], q_rs.at[t, p], q_ss.at[t, k], {"seq": p})
        query = q_all[t, 0]
        for i in range(1, SEQ):
            query += q_all[t, i]
        query = query.astype(jnp.bfloat16).astype(jnp.float32)
        spread = jnp.concatenate(
            [jnp.where(col_head == h, query, 0.0) for h in range(4)], axis=0
        ).astype(jnp.bfloat16)
        scores = lax.dot_general(
            spread, keys[...], (((1,), (1,)), ((), ())), preferred_element_type=jnp.float32
        ) * 0.125
        top = jnp.max(scores, axis=-1, keepdims=True)
        expo = jnp.exp(scores - top)
        total = jnp.sum(expo, axis=-1, keepdims=True)
        mixed = jnp.dot(expo.astype(jnp.bfloat16), vals[...], preferred_element_type=jnp.float32)
        ctx = jnp.zeros((BEAMS, 256), jnp.float32)
        stats = jnp.zeros((8, 128), jnp.float32)
        for h in range(4):
            ctx += jnp.where(col_head == h, mixed[16 * h:16 * h + 16], 0.0)
            for half in range(2):
                at = 16 * h + 8 * half
                stats = jnp.where(lane == 8 * half + h, top[at:at + 8], stats)
                stats = jnp.where(lane == 8 * half + 4 + h, total[at:at + 8], stats)
        ctx = ctx.astype(jnp.bfloat16)
        c_own[t] = ctx
        t_own[t] = stats
        c_all[t, s] = ctx
        t_all[t, s] = stats
        for k, p in enumerate(seq_peers):
            send(t_own.at[t], t_all.at[t, s], t_ss.at[t, k], t_rs.at[t, s], {"seq": p})
            send(c_own.at[t], c_all.at[t, s], c_ss.at[t, k], c_rs.at[t, s], {"seq": p})
        for k, p in enumerate(seq_peers):
            arrived(t_all.at[t, p], t_rs.at[t, p], t_ss.at[t, k], {"seq": p})
            arrived(c_all.at[t, p], c_rs.at[t, p], c_ss.at[t, k], {"seq": p})
        each = [t_all[t, i] for i in range(SEQ)]
        peak = functools.reduce(jnp.maximum, each)
        factors = [jnp.exp(one - peak) for one in each]
        sums = functools.reduce(
            lambda a, b: a + b, [f * pltpu.roll(one, 124, 1) for f, one in zip(factors, each)]
        )
        halves = []
        for half in range(2):
            acc = jnp.zeros((8, 256), jnp.float32)
            for i in range(SEQ):
                share = factors[i] / sums
                scale = jnp.zeros((8, 256), jnp.float32)
                for h in range(4):
                    at = 8 * half + h
                    scale = jnp.where(
                        col_head[:8] == h, jnp.broadcast_to(share[:, at:at + 1], (8, 256)), scale
                    )
                acc += c_all[t, i].astype(jnp.float32)[8 * half:8 * half + 8] * scale
            halves.append(acc)
        context = jnp.concatenate(halves, axis=0).astype(jnp.bfloat16)
        partial = jnp.dot(context, wo[...], preferred_element_type=jnp.float32)
        for j in range(4):
            p_own[t, :, j, :] = partial[:, 128 * j:128 * j + 128]
        p_all[t, c] = p_own[t, c]
        for k, p in enumerate(head_peers):
            send(p_own.at[t, p], p_all.at[t, c], p_ss.at[t, k], p_rs.at[t, c], {"head": p})
        for k, p in enumerate(head_peers):
            arrived(p_all.at[t, p], p_rs.at[t, p], p_ss.at[t, k], {"head": p})
        row = p_all[t, 0]
        for i in range(1, HEAD):
            row += p_all[t, i]
        f_own[t] = row
        f_all[t, s] = row
        for k, p in enumerate(seq_peers):
            send(f_own.at[t], f_all.at[t, s], f_ss.at[t, k], f_rs.at[t, s], {"seq": p})
        for k, p in enumerate(seq_peers):
            arrived(f_all.at[t, p], f_rs.at[t, p], f_ss.at[t, k], {"seq": p})
        for k, p in enumerate(head_peers):
            send(f_all.at[t], g_all.at[t, c], g_ss.at[t, k], g_rs.at[t, c], {"head": p})
        g_all[t, c] = f_all[t]
        for k, p in enumerate(head_peers):
            arrived(g_all.at[t, p], g_rs.at[t, p], g_ss.at[t, k], {"head": p})
        for b in range(BEAMS):
            state[t, b] = state[t, b] + g_all[t, b]
    for b in range(BEAMS):
        out_state[b] = state[STEPS - 1, b]
        out_att[b] = g_all[0, b] + g_all[1, b]
    for copy in sent:
        copy.wait_send()


def decode(keys, values, wq, wo, gain, first, parents, tokens):
    vmem = pl.BlockSpec(memory_space=pltpu.VMEM)
    f32, bf16 = jnp.float32, jnp.bfloat16
    dma = pltpu.SemaphoreType.DMA
    rows = jax.ShapeDtypeStruct((BEAMS, 8, 4, 128), f32)
    return pl.pallas_call(
        decode_kernel,
        out_shape=(rows, rows),
        in_specs=[vmem] * 6 + [pl.BlockSpec(memory_space=pltpu.SMEM), vmem],
        out_specs=(vmem, vmem),
        scratch_shapes=[
            pltpu.VMEM((STEPS, BEAMS, 8, 4, 128), f32),
            pltpu.VMEM((BEAMS, 8, 4, 128), f32),
            pltpu.VMEM((STEPS, BEAMS, 256), f32),
            pltpu.VMEM((STEPS, SEQ, BEAMS, 256), f32),
            pltpu.VMEM((STEPS, BEAMS, 256), bf16),
            pltpu.VMEM((STEPS, SEQ, BEAMS, 256), bf16),
            pltpu.VMEM((STEPS, 8, 128), f32),
            pltpu.VMEM((STEPS, SEQ, 8, 128), f32),
            pltpu.VMEM((STEPS, BEAMS, 4, 128), f32),
            pltpu.VMEM((STEPS, HEAD, 4, 128), f32),
            pltpu.VMEM((STEPS, 4, 128), f32),
            pltpu.VMEM((STEPS, SEQ, 4, 128), f32),
            pltpu.VMEM((STEPS, BEAMS, 8, 4, 128), f32),
            dma((STEPS, SEQ)), dma((STEPS, SEQ)),
            dma((STEPS, SEQ)), dma((STEPS, SEQ)),
            dma((STEPS, SEQ)), dma((STEPS, SEQ)),
            dma((STEPS, HEAD)), dma((STEPS, HEAD)),
            dma((STEPS, SEQ)), dma((STEPS, SEQ)),
            dma((STEPS, HEAD)), dma((STEPS, HEAD)),
        ],
        compiler_params=pltpu.CompilerParams(collective_id=1, has_side_effects=True),
        name="decode",
    )(keys, values, wq, wo, gain, first, parents, tokens)


def on_device(
    enc_out, enc_gain, key_weight, value_weight, query_weight, out_weight,
    dec_gain, beam_state, parents, token_embed,
):
    full_rows = lax.all_gather(enc_out, "head", axis=1, tiled=True)
    memory = rms_norm(full_rows.astype(jnp.float32), enc_gain).astype(jnp.bfloat16)
    key_full = lax.all_gather(key_weight, "seq", axis=0, tiled=True)
    value_full = lax.all_gather(value_weight, "seq", axis=0, tiled=True)
    keys = jnp.dot(memory, key_full, preferred_element_type=jnp.float32).astype(jnp.bfloat16)
    values = jnp.dot(memory, value_full, preferred_element_type=jnp.float32).astype(jnp.bfloat16)
    state, attended = decode(
        keys, values, query_weight, out_weight,
        dec_gain.reshape(8, 4, 128),
        beam_state.reshape(BEAMS, 8, 4, 128),
        parents,
        token_embed.astype(jnp.float32).reshape(STEPS, BEAMS, 8, 4, 128),
    )
    return state.reshape(BEAMS, 4096), attended.reshape(BEAMS, 4096)


def solution(mesh):
    placed = (
        P(("src", "seq"), "head"),
        P(),
        P("seq", "head"),
        P("seq", "head"),
        P("seq", "head"),
        P("head", "seq"),
        P(),
        P("src", None),
        P("src", None),
        P("src", None, None),
    )
    return jax.shard_map(
        on_device,
        mesh=mesh,
        in_specs=placed,
        out_specs=(P("src", None), P("src", None)),
        check_vma=False,
    )
```

```python
import functools

import jax
import jax.numpy as jnp
from jax import lax
from jax.experimental import pallas as pl
from jax.experimental.pallas import tpu as pltpu
from jax.sharding import PartitionSpec as P

MESH = pl.DeviceIdType.MESH
HEAD_DIM = 64
BEAMS = 16
STEPS = 2
SEQ = 8
HEAD = 16


def place():
    y = lax.axis_index("src")
    s = lax.axis_index("seq")
    c = lax.axis_index("head")
    zh, k = lax.div(s, 2), lax.rem(s, 2)
    zl, x = lax.div(c, 4), lax.rem(c, 4)
    b, r = lax.rem(zl, 2), lax.div(zl, 2)
    return y, s, c, k, zl, x, b, r, zh * 2 + r


def node_id(m, k, b, x):
    return {"seq": lax.div(m, 2) * 2 + k, "head": (lax.rem(m, 2) * 2 + b) * 4 + x}


def partner_id(s, k):
    return {"seq": s + 1 - 2 * k}


def start_send(sent, src, dst, ss, rs, where):
    copy = pltpu.make_async_remote_copy(
        src_ref=src, dst_ref=dst, send_sem=ss, recv_sem=rs, device_id=where, device_id_type=MESH,
    )
    copy.start()
    sent.append(copy)


def wait_arrival(dst, ss, rs, where):
    pltpu.make_async_remote_copy(
        src_ref=dst, dst_ref=dst, send_sem=ss, recv_sem=rs, device_id=where, device_id_type=MESH,
    ).wait_recv()


OFFSETS = (0, -1, 1, -2, 2, -3, 3, 4)
BY_OFFSET = {off: q for q, off in enumerate(OFFSETS)}


def gather_kernel(
    enc, gain, wk, wv, out,
    ebuf, nbuf, wbuf,
    own_sem, wz_ss, wz_rs, wy_ss, wy_rs, wh_ss, wh_rs, wc_ss, wc_rs, ez_ss, ez_rs, ex_ss, ex_rs, eh_ss, eh_rs,
):
    y, s, c, k, zl, x, b, r, n = place()
    up, down = {"src": lax.rem(y + 1, 4)}, {"src": lax.rem(y + 3, 4)}
    east = {"head": zl * 4 + lax.rem(x + 1, 4)}
    west = {"head": zl * 4 + lax.rem(x + 3, 4)}
    partner = partner_id(s, k)
    right = node_id(lax.rem(n + 1, 8), k, b, x)
    left = node_id(lax.rem(n + 7, 8), k, b, x)
    sibling = zl + 1 - 2 * b
    across = [2 - 2 * r, 3 - 2 * r]
    quarters = [y, lax.rem(y + 3, 4), lax.rem(y + 1, 4), lax.rem(y + 2, 4)]

    def rows_of(m, quarter, core):
        return pl.ds(pl.multiple_of((lax.div(m, 2) * 2 + core) * 512 + quarter * 128, 128), 128)

    def nodes(q):
        return lax.rem(n + 8 + OFFSETS[q], 8)

    def both(q, j, core):
        m = nodes(q)
        return wbuf.at[pl.ds(2 * lax.rem(m, 2), 2), rows_of(m, quarters[j], core), :]

    def one(q, j, mat):
        m = nodes(q)
        return wbuf.at[2 * lax.rem(m, 2) + mat, rows_of(m, quarters[j], k), :]

    def local(src, dst, i):
        copy = pltpu.make_async_copy(src, dst, own_sem.at[i])
        copy.start()
        return copy

    mine = pl.ds(pl.multiple_of(y * 128, 128), 128)
    near = pl.ds(pl.multiple_of(r * 512, 512), 512)
    far = pl.ds(pl.multiple_of(512 - r * 512, 512), 512)
    locals_ = [
        local(wk.at[mine, :], one(0, 0, 0), 0),
        local(wv.at[mine, :], one(0, 0, 1), 1),
        local(enc.at[near, :], ebuf.at[c], 2),
    ]

    barrier = pltpu.get_barrier_semaphore()
    greet = [up, down, east, west, partner, right, left]
    greet += [{"head": zl_to * 4 + x} for zl_to in [sibling] + across]
    for where in greet:
        pl.semaphore_signal(barrier, inc=1, device_id=where, device_id_type=MESH)
    for copy in locals_:
        copy.wait()
    pl.semaphore_wait(barrier, len(greet))

    sent = []
    send = functools.partial(start_send, sent)

    def z_on(q):
        off = OFFSETS[q]
        if off <= 0 and off > -3:
            t = BY_OFFSET[off - 1]
            send(both(q, 0, k), both(q, 0, k), wz_ss.at[t], wz_rs.at[t], right)
        if off >= 0 and off < 3:
            t = BY_OFFSET[off + 1]
            send(both(q, 0, k), both(q, 0, k), wz_ss.at[t], wz_rs.at[t], left)
        if off == -3:
            send(one(q, 0, 0), one(q, 0, 0), wz_ss.at[7], wz_rs.at[7], right)
        if off == 3:
            send(one(q, 0, 1), one(q, 0, 1), wz_ss.at[8], wz_rs.at[8], left)

    def z_in(q):
        off = OFFSETS[q]
        if off == 4:
            wait_arrival(one(q, 0, 0), wz_ss.at[7], wz_rs.at[7], right)
            wait_arrival(one(q, 0, 1), wz_ss.at[8], wz_rs.at[8], left)
        else:
            wait_arrival(both(q, 0, k), wz_ss.at[q], wz_rs.at[q], right)

    def cross(q, j):
        send(both(q, j, k), both(q, j, k), wc_ss.at[q, j], wc_rs.at[q, j], partner)

    def y_out(q):
        send(both(q, 0, k), both(q, 0, k), wy_ss.at[q, 0], wy_rs.at[q, 0], up)
        send(both(q, 0, k), both(q, 0, k), wy_ss.at[q, 1], wy_rs.at[q, 1], down)
        cross(q, 0)

    def y_relay(q):
        wait_arrival(both(q, 1, k), wy_ss.at[q, 0], wy_rs.at[q, 0], up)
        send(one(q, 1, 0), one(q, 1, 0), wh_ss.at[q, 0], wh_rs.at[q, 0], up)
        cross(q, 1)
        wait_arrival(both(q, 2, k), wy_ss.at[q, 1], wy_rs.at[q, 1], down)
        send(one(q, 2, 1), one(q, 2, 1), wh_ss.at[q, 1], wh_rs.at[q, 1], down)
        cross(q, 2)

    def y_last(q):
        wait_arrival(one(q, 3, 0), wh_ss.at[q, 0], wh_rs.at[q, 0], up)
        wait_arrival(one(q, 3, 1), wh_ss.at[q, 1], wh_rs.at[q, 1], down)
        cross(q, 3)

    piece_z = [zl, sibling] + across

    def piece(p, xs):
        return ebuf.at[piece_z[p] * 4 + xs]

    xs = [x, lax.rem(x + 3, 4), lax.rem(x + 1, 4), lax.rem(x + 2, 4)]
    top_half, low_half = pl.ds(0, 256), pl.ds(256, 256)

    def x_out(p):
        send(piece(p, x), piece(p, x), ex_ss.at[p, 0], ex_rs.at[p, 0], east)
        send(piece(p, x), piece(p, x), ex_ss.at[p, 1], ex_rs.at[p, 1], west)

    def x_relay(p):
        wait_arrival(piece(p, xs[1]), ex_ss.at[p, 0], ex_rs.at[p, 0], east)
        part = piece(p, xs[1]).at[top_half, :]
        send(part, part, eh_ss.at[p, 0], eh_rs.at[p, 0], east)
        wait_arrival(piece(p, xs[2]), ex_ss.at[p, 1], ex_rs.at[p, 1], west)
        part = piece(p, xs[2]).at[low_half, :]
        send(part, part, eh_ss.at[p, 1], eh_rs.at[p, 1], west)

    def x_last(p):
        wait_arrival(piece(p, xs[3]).at[top_half, :], eh_ss.at[p, 0], eh_rs.at[p, 0], east)
        wait_arrival(piece(p, xs[3]).at[low_half, :], eh_ss.at[p, 1], eh_rs.at[p, 1], west)

    z_on(0)
    y_out(0)
    send(enc.at[far, :], ebuf.at[c], ez_ss.at[1], ez_rs.at[1 + b], {"head": across[0] * 4 + x})
    send(enc.at[far, :], ebuf.at[c], ez_ss.at[2], ez_rs.at[1 + b], {"head": across[1] * 4 + x})
    send(enc.at[near, :], ebuf.at[c], ez_ss.at[0], ez_rs.at[0], {"head": sibling * 4 + x})
    x_out(0)
    rounds = [[0], [1, 2], [3, 4], [5, 6], [7]]
    for h in range(1, 7):
        if h < 5:
            for q in rounds[h]:
                z_in(q)
                z_on(q)
                y_out(q)
        if h < 4:
            wait_arrival(piece(h, x), ez_ss.at[h - 1], ez_rs.at[h - 1], east)
            x_out(h)
        if h - 1 < 5:
            for q in rounds[h - 1]:
                y_relay(q)
        if h - 1 < 4:
            x_relay(h - 1)
        if h >= 2:
            for q in rounds[h - 2]:
                y_last(q)
            if h - 2 < 4:
                x_last(h - 2)
    for q in range(8):
        for j in range(4):
            wait_arrival(both(q, j, 1 - k), wc_ss.at[q, j], wc_rs.at[q, j], partner)

    @pl.loop(0, 8)
    def _(i):
        at = pl.ds(pl.multiple_of(i * 64, 64), 64)
        acc = jnp.zeros((64, 128), jnp.float32)
        for f in range(HEAD):
            part = ebuf[f, at, :].astype(jnp.float32)
            part = part * part
            acc += part[:, :128] + part[:, 128:]
        scale = lax.rsqrt(jnp.sum(acc, axis=-1, keepdims=True) * (1.0 / 4096.0) + 1e-06)
        for f in range(HEAD):
            part = ebuf[f, at, :].astype(jnp.float32) * scale * gain[f:f + 1, :]
            nbuf[at, 256 * f:256 * f + 256] = part.astype(jnp.bfloat16)

    @pl.loop(0, 4)
    def _(i):
        out[i] = jnp.dot(nbuf[...], wbuf[i], preferred_element_type=jnp.float32).astype(jnp.bfloat16)

    for copy in sent:
        copy.wait_send()


def gather(enc, gain, wk, wv):
    vmem = pl.BlockSpec(memory_space=pltpu.VMEM)
    bf16 = jnp.bfloat16
    dma = pltpu.SemaphoreType.DMA
    return pl.pallas_call(
        gather_kernel,
        out_shape=jax.ShapeDtypeStruct((4, 512, 256), bf16),
        in_specs=[vmem] * 4,
        out_specs=vmem,
        scratch_shapes=[
            pltpu.VMEM((HEAD, 512, 256), bf16),
            pltpu.VMEM((512, 4096), bf16),
            pltpu.VMEM((4, 4096, 256), bf16),
            dma((3,)),
            dma((9,)), dma((9,)),
            dma((8, 2)), dma((8, 2)),
            dma((8, 2)), dma((8, 2)),
            dma((8, 4)), dma((8, 4)),
            dma((3,)), dma((3,)),
            dma((4, 2)), dma((4, 2)),
            dma((4, 2)), dma((4, 2)),
        ],
        compiler_params=pltpu.CompilerParams(collective_id=2, has_side_effects=True),
        name="gather",
    )(enc, gain, wk, wv)


def decode_kernel(
    kv, wq, wo, gain, first, parents, tokens,
    out_state, out_att,
    state, nrm, q_own, q_all, u_own, u_all, c_own, c_all, t_own, t_all, m_own, m_all, v_own, v_all,
    p_own, p_all, f_own, f_all, g_all,
    q_ss, q_rs, u_ss, u_rs, c_ss, c_rs, t_ss, t_rs, m_ss, m_rs, v_ss, v_rs, p_ss, p_rs, f_ss, f_rs, g_ss, g_rs,
):
    y, s, c, k, zl, x, b, r, n = place()
    seq_peers = [lax.rem(s + i, SEQ) for i in range(1, SEQ)]
    head_peers = [lax.rem(c + i, HEAD) for i in range(1, HEAD)]
    ring_peers = [lax.rem(n + i, 8) for i in range(1, 8)]
    partner = partner_id(s, k)
    other = 1 - k

    def ring(m):
        return node_id(m, k, b, x)

    barrier = pltpu.get_barrier_semaphore()
    greet = [{"seq": p} for p in seq_peers] + [{"head": p} for p in head_peers]
    greet += [ring(m) for m in ring_peers]
    for where in greet:
        pl.semaphore_signal(barrier, inc=1, device_id=where, device_id_type=MESH)
    pl.semaphore_wait(barrier, len(greet))

    sent = []
    send = functools.partial(start_send, sent)

    col_head = lax.broadcasted_iota(jnp.int32, (BEAMS, 256), 1) // HEAD_DIM
    lane = lax.broadcasted_iota(jnp.int32, (8, 128), 1)

    def spread_rows(share):
        halves = []
        for half in range(2):
            scale = jnp.zeros((8, 256), jnp.float32)
            for h in range(4):
                at = 8 * half + h
                scale = jnp.where(
                    col_head[:8] == h, jnp.broadcast_to(share[:, at:at + 1], (8, 256)), scale
                )
            halves.append(scale)
        return jnp.concatenate(halves, axis=0)

    def merge(stats, parts):
        peak = functools.reduce(jnp.maximum, stats)
        factors = [jnp.exp(one - peak) for one in stats]
        sums = functools.reduce(
            lambda a, b: a + b, [f * pltpu.roll(one, 124, 1) for f, one in zip(factors, stats)]
        )
        joined = functools.reduce(
            lambda a, b: a + b, [part * spread_rows(f) for f, part in zip(factors, parts)]
        )
        return peak, sums, joined

    is_top = lax.rem(lane, 8) < 4

    for t in range(STEPS):
        for i in range(BEAMS):
            source = first[parents[t, i]] if t == 0 else state[t - 1, parents[t, i]]
            row = source + tokens[t, i]
            square = jnp.sum(jnp.sum(row * row, axis=0), axis=(0, 1), keepdims=True) * (1.0 / 4096.0)
            state[t, i] = row
            nrm[i] = row * lax.rsqrt(square + 1e-06)[None] * gain[...]
        part = jnp.zeros((BEAMS, 256), jnp.float32)
        for j in range(4):
            part += jnp.dot(
                nrm[:, s, j, :].astype(jnp.bfloat16), wq[pl.ds(128 * j, 128), :],
                preferred_element_type=jnp.float32,
            )
        q_own[t] = part
        q_all[t, n] = part
        for i, m in enumerate(ring_peers):
            send(q_own.at[t], q_all.at[t, n], q_ss.at[t, i], q_rs.at[t, n], ring(m))
        for i, m in enumerate(ring_peers):
            wait_arrival(q_all.at[t, m], q_ss.at[t, i], q_rs.at[t, m], ring(m))
        for g in range(2):
            u_all[t, k, g] = (q_all[t, g] + q_all[t, g + 2]) + (q_all[t, g + 4] + q_all[t, g + 6])
            u_own[t, g] = u_all[t, k, g]
        send(u_own.at[t], u_all.at[t, k], u_ss.at[t], u_rs.at[t], partner)
        wait_arrival(u_all.at[t, other], u_ss.at[t], u_rs.at[t], partner)
        for g in range(2):
            query = (u_all[t, 0, g] + u_all[t, 1, g]).astype(jnp.bfloat16).astype(jnp.float32)
            spread = jnp.concatenate(
                [jnp.where(col_head == h, query, 0.0) for h in range(4)], axis=0
            ).astype(jnp.bfloat16)
            scores = lax.dot_general(
                spread, kv[2 * g], (((1,), (1,)), ((), ())), preferred_element_type=jnp.float32
            ) * 0.125
            top = jnp.max(scores, axis=-1, keepdims=True)
            expo = jnp.exp(scores - top)
            total = jnp.sum(expo, axis=-1, keepdims=True)
            mixed = jnp.dot(
                expo.astype(jnp.bfloat16), kv[2 * g + 1], preferred_element_type=jnp.float32
            )
            ctx = jnp.zeros((BEAMS, 256), jnp.float32)
            stats = jnp.zeros((8, 128), jnp.float32)
            for h in range(4):
                ctx += jnp.where(col_head == h, mixed[16 * h:16 * h + 16], 0.0)
                for half in range(2):
                    at = 16 * h + 8 * half
                    stats = jnp.where(lane == 8 * half + h, top[at:at + 8], stats)
                    stats = jnp.where(lane == 8 * half + 4 + h, total[at:at + 8], stats)
            c_own[t, g] = ctx.astype(jnp.bfloat16)
            t_own[t, g] = stats
        c_all[t, n] = c_own[t, r]
        t_all[t, n] = t_own[t, r]
        for i, m in enumerate(ring_peers):
            g = lax.rem(m, 2)
            send(t_own.at[t, g], t_all.at[t, n], t_ss.at[t, i], t_rs.at[t, n], ring(m))
            send(c_own.at[t, g], c_all.at[t, n], c_ss.at[t, i], c_rs.at[t, n], ring(m))
        for i, m in enumerate(ring_peers):
            wait_arrival(t_all.at[t, m], t_ss.at[t, i], t_rs.at[t, m], ring(m))
            wait_arrival(c_all.at[t, m], c_ss.at[t, i], c_rs.at[t, m], ring(m))
        peak, sums, joined = merge(
            [t_all[t, i] for i in range(8)], [c_all[t, i].astype(jnp.float32) for i in range(8)]
        )
        stats = jnp.where(is_top, peak, pltpu.roll(sums, 4, 1))
        v_own[t] = joined
        m_own[t] = stats
        v_all[t, k] = joined
        m_all[t, k] = stats
        send(m_own.at[t], m_all.at[t, k], m_ss.at[t], m_rs.at[t], partner)
        send(v_own.at[t], v_all.at[t, k], v_ss.at[t], v_rs.at[t], partner)
        wait_arrival(m_all.at[t, other], m_ss.at[t], m_rs.at[t], partner)
        wait_arrival(v_all.at[t, other], v_ss.at[t], v_rs.at[t], partner)
        peak, sums, joined = merge([m_all[t, 0], m_all[t, 1]], [v_all[t, 0], v_all[t, 1]])
        context = (joined / spread_rows(sums)).astype(jnp.bfloat16)
        partial = jnp.dot(context, wo[...], preferred_element_type=jnp.float32)
        for j in range(4):
            p_own[t, :, j, :] = partial[:, 128 * j:128 * j + 128]
        p_all[t, c] = p_own[t, c]
        for i, p in enumerate(head_peers):
            send(p_own.at[t, p], p_all.at[t, c], p_ss.at[t, i], p_rs.at[t, c], {"head": p})
        for i, p in enumerate(head_peers):
            wait_arrival(p_all.at[t, p], p_ss.at[t, i], p_rs.at[t, p], {"head": p})
        row = p_all[t, 0]
        for i in range(1, HEAD):
            row += p_all[t, i]
        f_own[t] = row
        f_all[t, s] = row
        for i, p in enumerate(seq_peers):
            send(f_own.at[t], f_all.at[t, s], f_ss.at[t, i], f_rs.at[t, s], {"seq": p})
        for i, p in enumerate(seq_peers):
            wait_arrival(f_all.at[t, p], f_ss.at[t, i], f_rs.at[t, p], {"seq": p})
        for i, p in enumerate(head_peers):
            send(f_all.at[t], g_all.at[t, c], g_ss.at[t, i], g_rs.at[t, c], {"head": p})
        g_all[t, c] = f_all[t]
        for i, p in enumerate(head_peers):
            wait_arrival(g_all.at[t, p], g_ss.at[t, i], g_rs.at[t, p], {"head": p})
        for i in range(BEAMS):
            state[t, i] = state[t, i] + g_all[t, i]
    for i in range(BEAMS):
        out_state[i] = state[STEPS - 1, i]
        out_att[i] = g_all[0, i] + g_all[1, i]
    for copy in sent:
        copy.wait_send()


def decode(kv, wq, wo, gain, first, parents, tokens):
    vmem = pl.BlockSpec(memory_space=pltpu.VMEM)
    f32, bf16 = jnp.float32, jnp.bfloat16
    dma = pltpu.SemaphoreType.DMA
    rows = jax.ShapeDtypeStruct((BEAMS, 8, 4, 128), f32)
    return pl.pallas_call(
        decode_kernel,
        out_shape=(rows, rows),
        in_specs=[vmem] * 5 + [pl.BlockSpec(memory_space=pltpu.SMEM), vmem],
        out_specs=(vmem, vmem),
        scratch_shapes=[
            pltpu.VMEM((STEPS, BEAMS, 8, 4, 128), f32),
            pltpu.VMEM((BEAMS, 8, 4, 128), f32),
            pltpu.VMEM((STEPS, BEAMS, 256), f32),
            pltpu.VMEM((STEPS, 8, BEAMS, 256), f32),
            pltpu.VMEM((STEPS, 2, BEAMS, 256), f32),
            pltpu.VMEM((STEPS, 2, 2, BEAMS, 256), f32),
            pltpu.VMEM((STEPS, 2, BEAMS, 256), bf16),
            pltpu.VMEM((STEPS, 8, BEAMS, 256), bf16),
            pltpu.VMEM((STEPS, 2, 8, 128), f32),
            pltpu.VMEM((STEPS, 8, 8, 128), f32),
            pltpu.VMEM((STEPS, 8, 128), f32),
            pltpu.VMEM((STEPS, 2, 8, 128), f32),
            pltpu.VMEM((STEPS, BEAMS, 256), f32),
            pltpu.VMEM((STEPS, 2, BEAMS, 256), f32),
            pltpu.VMEM((STEPS, BEAMS, 4, 128), f32),
            pltpu.VMEM((STEPS, HEAD, 4, 128), f32),
            pltpu.VMEM((STEPS, 4, 128), f32),
            pltpu.VMEM((STEPS, SEQ, 4, 128), f32),
            pltpu.VMEM((STEPS, BEAMS, 8, 4, 128), f32),
            dma((STEPS, 8)), dma((STEPS, 8)),
            dma((STEPS,)), dma((STEPS,)),
            dma((STEPS, 8)), dma((STEPS, 8)),
            dma((STEPS, 8)), dma((STEPS, 8)),
            dma((STEPS,)), dma((STEPS,)),
            dma((STEPS,)), dma((STEPS,)),
            dma((STEPS, HEAD)), dma((STEPS, HEAD)),
            dma((STEPS, SEQ)), dma((STEPS, SEQ)),
            dma((STEPS, HEAD)), dma((STEPS, HEAD)),
        ],
        compiler_params=pltpu.CompilerParams(collective_id=1, has_side_effects=True),
        name="decode",
    )(kv, wq, wo, gain, first, parents, tokens)


def on_device(
    enc_out, enc_gain, key_weight, value_weight, query_weight, out_weight,
    dec_gain, beam_state, parents, token_embed,
):
    kv = gather(enc_out, enc_gain.reshape(HEAD, 256), key_weight, value_weight)
    state, attended = decode(
        kv, query_weight, out_weight,
        dec_gain.reshape(8, 4, 128),
        beam_state.reshape(BEAMS, 8, 4, 128),
        parents,
        token_embed.astype(jnp.float32).reshape(STEPS, BEAMS, 8, 4, 128),
    )
    return state.reshape(BEAMS, 4096), attended.reshape(BEAMS, 4096)


def solution(mesh):
    placed = (
        P(("src", "seq"), "head"),
        P(),
        P("seq", "head"),
        P("seq", "head"),
        P("seq", "head"),
        P("head", "seq"),
        P(),
        P("src", None),
        P("src", None),
        P("src", None, None),
    )
    return jax.shard_map(
        on_device,
        mesh=mesh,
        in_specs=placed,
        out_specs=(P("src", None), P("src", None)),
        check_vma=False,
    )
```

```python
import functools

import jax
import jax.numpy as jnp
from jax import lax
from jax.experimental import pallas as pl
from jax.experimental.pallas import tpu as pltpu
from jax.sharding import PartitionSpec as P

MESH = pl.DeviceIdType.MESH
HEAD_DIM = 64
BEAMS = 16
STEPS = 2
SEQ = 8
HEAD = 16


def place():
    y = lax.axis_index("src")
    s = lax.axis_index("seq")
    c = lax.axis_index("head")
    zh, k = lax.div(s, 2), lax.rem(s, 2)
    zl, x = lax.div(c, 4), lax.rem(c, 4)
    b, r = lax.rem(zl, 2), lax.div(zl, 2)
    return y, s, c, k, zl, x, b, r, zh * 2 + r


def node_id(m, k, b, x):
    return {"seq": lax.div(m, 2) * 2 + k, "head": (lax.rem(m, 2) * 2 + b) * 4 + x}


def partner_id(s, k):
    return {"seq": s + 1 - 2 * k}


def start_send(sent, src, dst, ss, rs, where):
    copy = pltpu.make_async_remote_copy(
        src_ref=src, dst_ref=dst, send_sem=ss, recv_sem=rs, device_id=where, device_id_type=MESH,
    )
    copy.start()
    sent.append(copy)


def wait_arrival(dst, ss, rs, where):
    pltpu.make_async_remote_copy(
        src_ref=dst, dst_ref=dst, send_sem=ss, recv_sem=rs, device_id=where, device_id_type=MESH,
    ).wait_recv()


OFFSETS = (0, -1, 1, -2, 2, -3, 3, 4)
BY_OFFSET = {off: q for q, off in enumerate(OFFSETS)}


def kernel(
    enc, enc_gain, wk, wv, wq, wo, gain, first, parents, tokens,
    out_state, out_att,
    ebuf, nbuf, wbuf, kv,
    pre, part, picked, local_rows, full,
    q_own, q_all, u_own, u_all, z_own, z_all, zz_own, zz_all, c_own, c_all, t_own, t_all, m_own, m_all, v_own, v_all,
    p_own, p_all, f_own, f_all, l_all, g_all,
    own_sem, wz_ss, wz_rs, wy_ss, wy_rs, wh_ss, wh_rs, wc_ss, wc_rs, ez_ss, ez_rs, ex_ss, ex_rs, eh_ss, eh_rs,
    q_ss, q_rs, u_ss, u_rs, z_ss, z_rs, zz_ss, zz_rs, c_ss, c_rs, t_ss, t_rs, m_ss, m_rs, v_ss, v_rs,
    p_ss, p_rs, f_ss, f_rs, l_ss, l_rs, g_ss, g_rs,
):
    y, s, c, k, zl, x, b, r, n = place()
    up, down = {"src": lax.rem(y + 1, 4)}, {"src": lax.rem(y + 3, 4)}
    east = {"head": zl * 4 + lax.rem(x + 1, 4)}
    west = {"head": zl * 4 + lax.rem(x + 3, 4)}
    partner = partner_id(s, k)
    right = node_id(lax.rem(n + 1, 8), k, b, x)
    left = node_id(lax.rem(n + 7, 8), k, b, x)
    sibling = zl + 1 - 2 * b
    opposite = lax.rem(zl + 2, 4)
    quarters = [y, lax.rem(y + 3, 4), lax.rem(y + 1, 4), lax.rem(y + 2, 4)]

    def rows_of(m, quarter, core):
        return pl.ds(pl.multiple_of((lax.div(m, 2) * 2 + core) * 512 + quarter * 128, 128), 128)

    def nodes(q):
        return lax.rem(n + 8 + OFFSETS[q], 8)

    def both(q, j, core):
        m = nodes(q)
        return wbuf.at[pl.ds(2 * lax.rem(m, 2), 2), rows_of(m, quarters[j], core), :]

    def one(q, j, mat):
        m = nodes(q)
        return wbuf.at[2 * lax.rem(m, 2) + mat, rows_of(m, quarters[j], k), :]

    def local(src, dst, i):
        copy = pltpu.make_async_copy(src, dst, own_sem.at[i])
        copy.start()
        return copy

    mine = pl.ds(pl.multiple_of(y * 128, 128), 128)
    near = pl.ds(pl.multiple_of(r * 512, 512), 512)
    far = pl.ds(pl.multiple_of(512 - r * 512, 512), 512)
    locals_ = [
        local(wk.at[mine, :], one(0, 0, 0), 0),
        local(wv.at[mine, :], one(0, 0, 1), 1),
        local(enc.at[near, :], ebuf.at[c], 2),
    ]

    seq_peers = [lax.rem(s + i, SEQ) for i in range(1, SEQ)]
    head_peers = [lax.rem(c + i, HEAD) for i in range(1, HEAD)]
    ring_peers = [lax.rem(n + i, 8) for i in range(1, 8)]
    other = 1 - k
    feats = pl.ds(pl.multiple_of(s * 512, 512), 512)

    def ring(m):
        return node_id(m, k, b, x)

    barrier = pltpu.get_barrier_semaphore()
    greet = [up, down]
    greet += [{"seq": p} for p in seq_peers] + [{"head": p} for p in head_peers]
    greet += [ring(m) for m in ring_peers]
    for where in greet:
        pl.semaphore_signal(barrier, inc=1, device_id=where, device_id_type=MESH)
    for copy in locals_:
        copy.wait()
    pl.semaphore_wait(barrier, len(greet))

    sent = []
    send = functools.partial(start_send, sent)

    def z_on(q):
        off = OFFSETS[q]
        if off <= 0 and off > -3:
            t = BY_OFFSET[off - 1]
            send(both(q, 0, k), both(q, 0, k), wz_ss.at[t], wz_rs.at[t], right)
        if off >= 0 and off < 3:
            t = BY_OFFSET[off + 1]
            send(both(q, 0, k), both(q, 0, k), wz_ss.at[t], wz_rs.at[t], left)
        if off == -3:
            send(one(q, 0, 0), one(q, 0, 0), wz_ss.at[7], wz_rs.at[7], right)
        if off == 3:
            send(one(q, 0, 1), one(q, 0, 1), wz_ss.at[8], wz_rs.at[8], left)

    def z_in(q):
        off = OFFSETS[q]
        if off == 4:
            wait_arrival(one(q, 0, 0), wz_ss.at[7], wz_rs.at[7], right)
            wait_arrival(one(q, 0, 1), wz_ss.at[8], wz_rs.at[8], left)
        else:
            wait_arrival(both(q, 0, k), wz_ss.at[q], wz_rs.at[q], right)

    def cross(q, j):
        send(both(q, j, k), both(q, j, k), wc_ss.at[q, j], wc_rs.at[q, j], partner)

    def y_out(q):
        send(both(q, 0, k), both(q, 0, k), wy_ss.at[q, 0], wy_rs.at[q, 0], up)
        send(both(q, 0, k), both(q, 0, k), wy_ss.at[q, 1], wy_rs.at[q, 1], down)
        cross(q, 0)

    def y_relay(q):
        wait_arrival(both(q, 1, k), wy_ss.at[q, 0], wy_rs.at[q, 0], up)
        send(one(q, 1, 0), one(q, 1, 0), wh_ss.at[q, 0], wh_rs.at[q, 0], up)
        cross(q, 1)
        wait_arrival(both(q, 2, k), wy_ss.at[q, 1], wy_rs.at[q, 1], down)
        send(one(q, 2, 1), one(q, 2, 1), wh_ss.at[q, 1], wh_rs.at[q, 1], down)
        cross(q, 2)

    def y_last(q):
        wait_arrival(one(q, 3, 0), wh_ss.at[q, 0], wh_rs.at[q, 0], up)
        wait_arrival(one(q, 3, 1), wh_ss.at[q, 1], wh_rs.at[q, 1], down)
        cross(q, 3)

    piece_z = [zl, sibling, opposite, lax.rem(sibling + 2, 4)]

    def piece(p, xs):
        return ebuf.at[piece_z[p] * 4 + xs]

    xs = [x, lax.rem(x + 3, 4), lax.rem(x + 1, 4), lax.rem(x + 2, 4)]
    top_half, low_half = pl.ds(0, 256), pl.ds(256, 256)

    def x_out(p):
        send(piece(p, x), piece(p, x), ex_ss.at[p, 0], ex_rs.at[p, 0], east)
        send(piece(p, x), piece(p, x), ex_ss.at[p, 1], ex_rs.at[p, 1], west)

    def x_relay(p):
        wait_arrival(piece(p, xs[1]), ex_ss.at[p, 0], ex_rs.at[p, 0], east)
        part = piece(p, xs[1]).at[top_half, :]
        send(part, part, eh_ss.at[p, 0], eh_rs.at[p, 0], east)
        wait_arrival(piece(p, xs[2]), ex_ss.at[p, 1], ex_rs.at[p, 1], west)
        part = piece(p, xs[2]).at[low_half, :]
        send(part, part, eh_ss.at[p, 1], eh_rs.at[p, 1], west)

    def x_last(p):
        wait_arrival(piece(p, xs[3]).at[top_half, :], eh_ss.at[p, 0], eh_rs.at[p, 0], east)
        wait_arrival(piece(p, xs[3]).at[low_half, :], eh_ss.at[p, 1], eh_rs.at[p, 1], west)

    col_head = lax.broadcasted_iota(jnp.int32, (BEAMS, 256), 1) // HEAD_DIM
    lane = lax.broadcasted_iota(jnp.int32, (8, 128), 1)
    is_top = lax.rem(lane, 8) < 4

    def spread_rows(share):
        halves = []
        for half in range(2):
            scale = jnp.zeros((8, 256), jnp.float32)
            for h in range(4):
                at = 8 * half + h
                scale = jnp.where(
                    col_head[:8] == h, jnp.broadcast_to(share[:, at:at + 1], (8, 256)), scale
                )
            halves.append(scale)
        return jnp.concatenate(halves, axis=0)

    def merge(stats, parts):
        peak = functools.reduce(jnp.maximum, stats)
        factors = [jnp.exp(one - peak) for one in stats]
        sums = functools.reduce(
            lambda a, b: a + b, [f * pltpu.roll(one, 124, 1) for f, one in zip(factors, stats)]
        )
        joined = functools.reduce(
            lambda a, b: a + b, [one * spread_rows(f) for f, one in zip(factors, parts)]
        )
        return peak, sums, joined

    def query_out(t):
        for i, m in enumerate(ring_peers):
            if t == 1:
                send(z_own, z_all.at[n], z_ss.at[i], z_rs.at[n], ring(m))
            send(q_own.at[t], q_all.at[t, n], q_ss.at[t, i], q_rs.at[t, n], ring(m))

    def query_swap(t):
        for i, m in enumerate(ring_peers):
            if t == 1:
                wait_arrival(z_all.at[m], z_ss.at[i], z_rs.at[m], ring(m))
            wait_arrival(q_all.at[t, m], q_ss.at[t, i], q_rs.at[t, m], ring(m))
        if t == 1:
            squares = (z_all[0] + z_all[2]) + (z_all[4] + z_all[6])
            zz_own[...] = squares
            zz_all[k] = squares
            send(zz_own, zz_all.at[k], zz_ss.at[0], zz_rs.at[0], partner)
        for g in range(2):
            both_g = (q_all[t, g] + q_all[t, g + 2]) + (q_all[t, g + 4] + q_all[t, g + 6])
            u_all[t, k, g] = both_g
            u_own[t, g] = both_g
        send(u_own.at[t], u_all.at[t, k], u_ss.at[t], u_rs.at[t], partner)

    def query_in(t):
        if t == 1:
            wait_arrival(zz_all.at[other], zz_ss.at[0], zz_rs.at[0], partner)
        wait_arrival(u_all.at[t, other], u_ss.at[t], u_rs.at[t], partner)

    def attend(t, g, scale):
        query = u_all[t, 0, g] + u_all[t, 1, g]
        if scale is not None:
            query = query * scale
        query = query.astype(jnp.bfloat16).astype(jnp.float32)
        spread = jnp.concatenate(
            [jnp.where(col_head == h, query, 0.0) for h in range(4)], axis=0
        ).astype(jnp.bfloat16)
        scores = lax.dot_general(
            spread, kv[2 * g], (((1,), (1,)), ((), ())), preferred_element_type=jnp.float32
        ) * 0.125
        top = jnp.max(scores, axis=-1, keepdims=True)
        expo = jnp.exp(scores - top)
        total = jnp.sum(expo, axis=-1, keepdims=True)
        mixed = jnp.dot(expo.astype(jnp.bfloat16), kv[2 * g + 1], preferred_element_type=jnp.float32)
        ctx = jnp.zeros((BEAMS, 256), jnp.float32)
        stats = jnp.zeros((8, 128), jnp.float32)
        for h in range(4):
            ctx += jnp.where(col_head == h, mixed[16 * h:16 * h + 16], 0.0)
            for half in range(2):
                at = 16 * h + 8 * half
                stats = jnp.where(lane == 8 * half + h, top[at:at + 8], stats)
                stats = jnp.where(lane == 8 * half + 4 + h, total[at:at + 8], stats)
        return ctx.astype(jnp.bfloat16), stats

    z_on(0)
    send(enc.at[near, :], ebuf.at[c], ez_ss.at[0], ez_rs.at[0], {"head": sibling * 4 + x})
    send(enc.at[far, :], ebuf.at[c], ez_ss.at[1], ez_rs.at[1], {"head": opposite * 4 + x})
    y_out(0)
    x_out(0)

    for i in range(BEAMS):
        picked[pl.ds(i, 1), :] = first[pl.ds(parents[0, i], 1), :]
    start = picked[...] + tokens[0].astype(jnp.float32)
    pre[...] = start
    mean = jnp.sum(start * start, axis=-1, keepdims=True) * (1.0 / 4096.0)
    picked[...] = start * lax.rsqrt(mean + 1e-06) * gain[...]
    q_own[0] = jnp.dot(picked[:, feats].astype(jnp.bfloat16), wq[...], preferred_element_type=jnp.float32)
    q_all[0, n] = q_own[0]
    query_out(0)

    def weights_round(qs):
        for q in qs:
            z_in(q)
            z_on(q)
            y_out(q)

    weights_round([1, 2])
    y_relay(0)
    x_relay(0)
    wait_arrival(piece(1, x), ez_ss.at[0], ez_rs.at[0], east)
    x_out(1)
    wait_arrival(piece(2, x), ez_ss.at[1], ez_rs.at[1], east)
    send(piece(2, x), piece(2, x), ez_ss.at[2], ez_rs.at[2], {"head": sibling * 4 + x})
    x_out(2)
    weights_round([3, 4])
    y_relay(1)
    y_relay(2)
    y_last(0)
    x_relay(1)
    x_last(0)
    weights_round([5, 6])
    wait_arrival(piece(3, x), ez_ss.at[2], ez_rs.at[2], east)
    x_out(3)
    y_relay(3)
    y_relay(4)
    x_relay(2)
    y_last(1)
    y_last(2)
    x_last(1)
    weights_round([7])
    query_swap(0)
    y_relay(5)
    y_relay(6)
    x_relay(3)
    y_last(3)
    y_last(4)
    x_last(2)
    y_relay(7)
    y_last(5)
    y_last(6)
    x_last(3)
    y_last(7)

    @pl.loop(0, 8)
    def _(i):
        at = pl.ds(pl.multiple_of(i * 64, 64), 64)
        acc = jnp.zeros((64, 128), jnp.float32)
        for f in range(HEAD):
            block = ebuf[f, at, :].astype(jnp.float32)
            block = block * block
            acc += block[:, :128] + block[:, 128:]
        scale = lax.rsqrt(jnp.sum(acc, axis=-1, keepdims=True) * (1.0 / 4096.0) + 1e-06)
        for f in range(HEAD):
            cols = slice(256 * f, 256 * f + 256)
            block = ebuf[f, at, :].astype(jnp.float32) * scale * enc_gain[:, cols]
            nbuf[at, cols] = block.astype(jnp.bfloat16)

    for q in range(8):
        for j in range(4):
            wait_arrival(both(q, j, other), wc_ss.at[q, j], wc_rs.at[q, j], partner)

    @pl.loop(0, 4)
    def _(i):
        kv[i] = jnp.dot(nbuf[...], wbuf[i], preferred_element_type=jnp.float32).astype(jnp.bfloat16)

    for t in range(STEPS):
        scale = None
        if t == 1:
            for j in range(4):
                part[:, 128 * j:128 * j + 128] = l_all[:, j, :]
            part[...] = part[...] + pre[:, feats]
            for i in range(BEAMS):
                local_rows[pl.ds(i, 1), :] = part[pl.ds(parents[1, i], 1), :]
            rows = local_rows[...] + tokens[1, :, feats].astype(jnp.float32)
            squares = jnp.sum(rows * rows, axis=-1, keepdims=True)
            z_own[...] = jnp.where(lane < 64, squares[:8], squares[8:])
            z_all[n] = z_own[...]
            scaled = rows * gain[:, feats]
            high = scaled.astype(jnp.bfloat16)
            low = (scaled - high.astype(jnp.float32)).astype(jnp.bfloat16)
            q_own[1] = jnp.dot(high, wq[...], preferred_element_type=jnp.float32) + jnp.dot(
                low, wq[...], preferred_element_type=jnp.float32
            )
            q_all[1, n] = q_own[1]
            query_out(1)
            query_swap(1)
            for i, p in enumerate(seq_peers):
                wait_arrival(f_all.at[0, p], f_ss.at[0, i], f_rs.at[0, p], {"seq": p})
            for i, p in enumerate(head_peers):
                send(f_all.at[0], g_all.at[0, c], g_ss.at[0, i], g_rs.at[0, c], {"head": p})
            g_all[0, c] = f_all[0]
        query_in(t)
        if t == 1:
            table = lax.rsqrt((zz_all[0] + zz_all[1]) * (1.0 / 4096.0) + 1e-06)
            scale = jnp.concatenate([table[:, :1], table[:, 64:65]], axis=0)
        ctx, stats = attend(t, 1 - r, scale)
        c_own[t, 0] = ctx
        t_own[t, 0] = stats
        for i in (0, 2, 4, 6):
            m = ring_peers[i]
            send(t_own.at[t, 0], t_all.at[t, n], t_ss.at[t, i], t_rs.at[t, n], ring(m))
            send(c_own.at[t, 0], c_all.at[t, n], c_ss.at[t, i], c_rs.at[t, n], ring(m))
        ctx, stats = attend(t, r, scale)
        c_own[t, 1] = ctx
        t_own[t, 1] = stats
        c_all[t, n] = ctx
        t_all[t, n] = stats
        for i in (1, 3, 5):
            m = ring_peers[i]
            send(t_own.at[t, 1], t_all.at[t, n], t_ss.at[t, i], t_rs.at[t, n], ring(m))
            send(c_own.at[t, 1], c_all.at[t, n], c_ss.at[t, i], c_rs.at[t, n], ring(m))
        if t == 1:
            for i, p in enumerate(head_peers):
                wait_arrival(g_all.at[0, p], g_ss.at[0, i], g_rs.at[0, p], {"head": p})
            for i in range(8):
                for j in range(4):
                    cols = slice(512 * i + 128 * j, 512 * i + 128 * j + 128)
                    one_col = g_all[0, :, i, j, :]
                    out_att[:, cols] = one_col
                    full[:, cols] = pre[:, cols] + one_col
            for i in range(BEAMS):
                picked[pl.ds(i, 1), :] = full[pl.ds(parents[1, i], 1), :]
            full[...] = picked[...] + tokens[1].astype(jnp.float32)
        for i, m in enumerate(ring_peers):
            wait_arrival(t_all.at[t, m], t_ss.at[t, i], t_rs.at[t, m], ring(m))
            wait_arrival(c_all.at[t, m], c_ss.at[t, i], c_rs.at[t, m], ring(m))
        peak, sums, joined = merge(
            [t_all[t, i] for i in range(8)], [c_all[t, i].astype(jnp.float32) for i in range(8)]
        )
        stats = jnp.where(is_top, peak, pltpu.roll(sums, 4, 1))
        v_own[t] = joined
        m_own[t] = stats
        v_all[t, k] = joined
        m_all[t, k] = stats
        send(m_own.at[t], m_all.at[t, k], m_ss.at[t], m_rs.at[t], partner)
        send(v_own.at[t], v_all.at[t, k], v_ss.at[t], v_rs.at[t], partner)
        wait_arrival(m_all.at[t, other], m_ss.at[t], m_rs.at[t], partner)
        wait_arrival(v_all.at[t, other], v_ss.at[t], v_rs.at[t], partner)
        peak, sums, joined = merge([m_all[t, 0], m_all[t, 1]], [v_all[t, 0], v_all[t, 1]])
        context = (joined / spread_rows(sums)).astype(jnp.bfloat16)
        partial = jnp.dot(context, wo[...], preferred_element_type=jnp.float32)
        for j in range(4):
            p_own[t, :, j, :] = partial[:, 128 * j:128 * j + 128]
        p_all[t, c] = p_own[t, c]
        for i, p in enumerate(head_peers):
            send(p_own.at[t, p], p_all.at[t, c], p_ss.at[t, i], p_rs.at[t, c], {"head": p})
        for i, p in enumerate(head_peers):
            wait_arrival(p_all.at[t, p], p_ss.at[t, i], p_rs.at[t, p], {"head": p})
        row = p_all[t, 0]
        for i in range(1, HEAD):
            row += p_all[t, i]
        f_own[t] = row
        f_all[t, s] = row
        if t == 0:
            for i, p in enumerate(head_peers):
                send(f_own.at[t], l_all.at[c], l_ss.at[i], l_rs.at[c], {"head": p})
            l_all[c] = row
        for i, p in enumerate(seq_peers):
            send(f_own.at[t], f_all.at[t, s], f_ss.at[t, i], f_rs.at[t, s], {"seq": p})
        if t == 0:
            for i, p in enumerate(head_peers):
                wait_arrival(l_all.at[p], l_ss.at[i], l_rs.at[p], {"head": p})
    for i, p in enumerate(seq_peers):
        wait_arrival(f_all.at[1, p], f_ss.at[1, i], f_rs.at[1, p], {"seq": p})
    for i, p in enumerate(head_peers):
        send(f_all.at[1], g_all.at[1, c], g_ss.at[1, i], g_rs.at[1, c], {"head": p})
    g_all[1, c] = f_all[1]
    for i, p in enumerate(head_peers):
        wait_arrival(g_all.at[1, p], g_ss.at[1, i], g_rs.at[1, p], {"head": p})
    for i in range(8):
        for j in range(4):
            cols = slice(512 * i + 128 * j, 512 * i + 128 * j + 128)
            one_col = g_all[1, :, i, j, :]
            out_state[:, cols] = full[:, cols] + one_col
            out_att[:, cols] = out_att[:, cols] + one_col
    for copy in sent:
        copy.wait_send()


def on_device(
    enc_out, enc_gain, key_weight, value_weight, query_weight, out_weight,
    dec_gain, beam_state, parents, token_embed,
):
    vmem = pl.BlockSpec(memory_space=pltpu.VMEM)
    f32, bf16 = jnp.float32, jnp.bfloat16
    dma = pltpu.SemaphoreType.DMA
    rows = jax.ShapeDtypeStruct((BEAMS, 4096), f32)

    def pair(*shape):
        return [dma(shape), dma(shape)]

    return pl.pallas_call(
        kernel,
        out_shape=(rows, rows),
        in_specs=[vmem] * 8 + [pl.BlockSpec(memory_space=pltpu.SMEM), vmem],
        out_specs=(vmem, vmem),
        scratch_shapes=[
            pltpu.VMEM((HEAD, 512, 256), bf16),
            pltpu.VMEM((512, 4096), bf16),
            pltpu.VMEM((4, 4096, 256), bf16),
            pltpu.VMEM((4, 512, 256), bf16),
            pltpu.VMEM((BEAMS, 4096), f32),
            pltpu.VMEM((BEAMS, 512), f32),
            pltpu.VMEM((BEAMS, 4096), f32),
            pltpu.VMEM((BEAMS, 512), f32),
            pltpu.VMEM((BEAMS, 4096), f32),
            pltpu.VMEM((STEPS, BEAMS, 256), f32),
            pltpu.VMEM((STEPS, 8, BEAMS, 256), f32),
            pltpu.VMEM((STEPS, 2, BEAMS, 256), f32),
            pltpu.VMEM((STEPS, 2, 2, BEAMS, 256), f32),
            pltpu.VMEM((8, 128), f32),
            pltpu.VMEM((8, 8, 128), f32),
            pltpu.VMEM((8, 128), f32),
            pltpu.VMEM((2, 8, 128), f32),
            pltpu.VMEM((STEPS, 2, BEAMS, 256), bf16),
            pltpu.VMEM((STEPS, 8, BEAMS, 256), bf16),
            pltpu.VMEM((STEPS, 2, 8, 128), f32),
            pltpu.VMEM((STEPS, 8, 8, 128), f32),
            pltpu.VMEM((STEPS, 8, 128), f32),
            pltpu.VMEM((STEPS, 2, 8, 128), f32),
            pltpu.VMEM((STEPS, BEAMS, 256), f32),
            pltpu.VMEM((STEPS, 2, BEAMS, 256), f32),
            pltpu.VMEM((STEPS, BEAMS, 4, 128), f32),
            pltpu.VMEM((STEPS, HEAD, 4, 128), f32),
            pltpu.VMEM((STEPS, 4, 128), f32),
            pltpu.VMEM((STEPS, SEQ, 4, 128), f32),
            pltpu.VMEM((BEAMS, 4, 128), f32),
            pltpu.VMEM((STEPS, BEAMS, 8, 4, 128), f32),
            dma((3,)),
            *pair(9), *pair(8, 2), *pair(8, 2), *pair(8, 4), *pair(3), *pair(4, 2), *pair(4, 2),
            *pair(STEPS, 8), *pair(STEPS), *pair(8), *pair(1), *pair(STEPS, 8), *pair(STEPS, 8),
            *pair(STEPS), *pair(STEPS), *pair(STEPS, HEAD), *pair(STEPS, SEQ), *pair(HEAD), *pair(STEPS, HEAD),
        ],
        compiler_params=pltpu.CompilerParams(collective_id=1, has_side_effects=True),
        name="beam_decode",
    )(
        enc_out, enc_gain.reshape(1, 4096), key_weight, value_weight, query_weight, out_weight,
        dec_gain.reshape(1, 4096), beam_state, parents, token_embed,
    )


def solution(mesh):
    placed = (
        P(("src", "seq"), "head"),
        P(),
        P("seq", "head"),
        P("seq", "head"),
        P("seq", "head"),
        P("head", "seq"),
        P(),
        P("src", None),
        P("src", None),
        P("src", None, None),
    )
    return jax.shard_map(
        on_device,
        mesh=mesh,
        in_specs=placed,
        out_specs=(P("src", None), P("src", None)),
        check_vma=False,
    )
```

```python
import functools

import jax
import jax.numpy as jnp
from jax import lax
from jax.experimental import pallas as pl
from jax.experimental.pallas import tpu as pltpu
from jax.sharding import PartitionSpec as P

MESH = pl.DeviceIdType.MESH
HEAD_DIM = 64
BEAMS = 16
STEPS = 2
SEQ = 8
HEAD = 16


def place():
    y = lax.axis_index("src")
    s = lax.axis_index("seq")
    c = lax.axis_index("head")
    zh, k = lax.div(s, 2), lax.rem(s, 2)
    zl, x = lax.div(c, 4), lax.rem(c, 4)
    b, r = lax.rem(zl, 2), lax.div(zl, 2)
    return y, s, c, k, zl, x, b, r, zh * 2 + r


def node_id(m, k, b, x):
    return {"seq": lax.div(m, 2) * 2 + k, "head": (lax.rem(m, 2) * 2 + b) * 4 + x}


def partner_id(s, k):
    return {"seq": s + 1 - 2 * k}


def start_send(sent, src, dst, ss, rs, where):
    copy = pltpu.make_async_remote_copy(
        src_ref=src, dst_ref=dst, send_sem=ss, recv_sem=rs, device_id=where, device_id_type=MESH,
    )
    copy.start()
    sent.append(copy)


def wait_arrival(dst, ss, rs, where):
    pltpu.make_async_remote_copy(
        src_ref=dst, dst_ref=dst, send_sem=ss, recv_sem=rs, device_id=where, device_id_type=MESH,
    ).wait_recv()


OFFSETS = (0, -1, 1, -2, 2, -3, 3, 4)
BY_OFFSET = {off: q for q, off in enumerate(OFFSETS)}


def kernel(
    enc, enc_gain, wk, wv, wq, wo, gain, first, parents, tokens,
    out_pre, out_first, out_second,
    ebuf, nbuf, wbuf, kv,
    pre, part, picked, local_rows, full,
    q_own, q_all, u_own, u_all, z_own, z_all, zz_own, zz_all, c_own, c_all, t_own, t_all, m_own, m_all, v_own, v_all,
    p_own, p_all, f_own, f_all, l_all, g_all,
    own_sem, wz_ss, wz_rs, wy_ss, wy_rs, wh_ss, wh_rs, wc_ss, wc_rs, ez_ss, ez_rs, ex_ss, ex_rs, eh_ss, eh_rs,
    q_ss, q_rs, u_ss, u_rs, z_ss, z_rs, zz_ss, zz_rs, c_ss, c_rs, t_ss, t_rs, m_ss, m_rs, v_ss, v_rs,
    p_ss, p_rs, f_ss, f_rs, l_ss, l_rs, g_ss, g_rs,
):
    y, s, c, k, zl, x, b, r, n = place()
    up, down = {"src": lax.rem(y + 1, 4)}, {"src": lax.rem(y + 3, 4)}
    east = {"head": zl * 4 + lax.rem(x + 1, 4)}
    west = {"head": zl * 4 + lax.rem(x + 3, 4)}
    partner = partner_id(s, k)
    right = node_id(lax.rem(n + 1, 8), k, b, x)
    left = node_id(lax.rem(n + 7, 8), k, b, x)
    sibling = zl + 1 - 2 * b
    opposite = lax.rem(zl + 2, 4)
    quarters = [y, lax.rem(y + 3, 4), lax.rem(y + 1, 4), lax.rem(y + 2, 4)]

    def rows_of(m, quarter, core):
        return pl.ds(pl.multiple_of((lax.div(m, 2) * 2 + core) * 512 + quarter * 128, 128), 128)

    def nodes(q):
        return lax.rem(n + 8 + OFFSETS[q], 8)

    def both(q, j, core):
        m = nodes(q)
        return wbuf.at[pl.ds(2 * lax.rem(m, 2), 2), rows_of(m, quarters[j], core), :]

    def one(q, j, mat):
        m = nodes(q)
        return wbuf.at[2 * lax.rem(m, 2) + mat, rows_of(m, quarters[j], k), :]

    def shard(mat):
        at = pl.ds(pl.multiple_of(s * 512, 512), 512)
        return wbuf.at[2 * r + mat, at, :]

    def shard_both(core):
        at = pl.ds(pl.multiple_of((lax.div(n, 2) * 2 + core) * 512, 512), 512)
        return wbuf.at[pl.ds(2 * r, 2), at, :]

    def local(src, dst, i):
        copy = pltpu.make_async_copy(src, dst, own_sem.at[i])
        copy.start()
        return copy

    near = pl.ds(pl.multiple_of(r * 512, 512), 512)
    far = pl.ds(pl.multiple_of(512 - r * 512, 512), 512)
    locals_ = [
        local(wk, shard(0), 0),
        local(wv, shard(1), 1),
        local(enc.at[near, :], ebuf.at[c], 2),
    ]
    seq_peers = [lax.rem(s + i, SEQ) for i in range(1, SEQ)]
    head_peers = [lax.rem(c + i, HEAD) for i in range(1, HEAD)]
    ring_peers = [lax.rem(n + i, 8) for i in range(1, 8)]
    other = 1 - k
    feats = pl.ds(pl.multiple_of(s * 512, 512), 512)

    def ring(m):
        return node_id(m, k, b, x)

    barrier = pltpu.get_barrier_semaphore()
    greet = [up, down]
    greet += [{"seq": p} for p in seq_peers] + [{"head": p} for p in head_peers]
    greet += [ring(m) for m in ring_peers]
    for where in greet:
        pl.semaphore_signal(barrier, inc=1, device_id=where, device_id_type=MESH)
    for copy in locals_:
        copy.wait()
    pl.semaphore_wait(barrier, len(greet))

    sent = []
    send = functools.partial(start_send, sent)

    def z_on(q, mat):
        off = OFFSETS[q]
        if -3 < off <= 0 or (off == -3 and mat == 0):
            t = 7 if off == -3 else BY_OFFSET[off - 1]
            send(one(q, 0, mat), one(q, 0, mat), wz_ss.at[t, mat], wz_rs.at[t, mat], right)
        if 0 <= off < 3 or (off == 3 and mat == 1):
            t = 7 if off == 3 else BY_OFFSET[off + 1]
            send(one(q, 0, mat), one(q, 0, mat), wz_ss.at[t, mat], wz_rs.at[t, mat], left)

    def z_step(q, mat):
        wait_arrival(one(q, 0, mat), wz_ss.at[q, mat], wz_rs.at[q, mat], right)
        z_on(q, mat)
        send(one(q, 0, mat), one(q, 0, mat), wy_ss.at[q, mat, 0], wy_rs.at[q, mat, 0], up)
        send(one(q, 0, mat), one(q, 0, mat), wy_ss.at[q, mat, 1], wy_rs.at[q, mat, 1], down)
        if mat == 1:
            cross(q, 0)

    def cross(q, j):
        send(both(q, j, k), both(q, j, k), wc_ss.at[q, j], wc_rs.at[q, j], partner)

    def y_relay(q):
        wait_arrival(one(q, 1, 0), wy_ss.at[q, 0, 0], wy_rs.at[q, 0, 0], up)
        send(one(q, 1, 0), one(q, 1, 0), wh_ss.at[q, 0], wh_rs.at[q, 0], up)
        wait_arrival(one(q, 2, 1), wy_ss.at[q, 1, 1], wy_rs.at[q, 1, 1], down)
        send(one(q, 2, 1), one(q, 2, 1), wh_ss.at[q, 1], wh_rs.at[q, 1], down)

    def y_cross(q):
        wait_arrival(one(q, 1, 1), wy_ss.at[q, 1, 0], wy_rs.at[q, 1, 0], up)
        cross(q, 1)
        wait_arrival(one(q, 2, 0), wy_ss.at[q, 0, 1], wy_rs.at[q, 0, 1], down)
        cross(q, 2)

    def y_last(q):
        wait_arrival(one(q, 3, 0), wh_ss.at[q, 0], wh_rs.at[q, 0], up)
        wait_arrival(one(q, 3, 1), wh_ss.at[q, 1], wh_rs.at[q, 1], down)
        cross(q, 3)

    piece_z = [zl, sibling, opposite, lax.rem(sibling + 2, 4)]
    xs = [x, lax.rem(x + 3, 4), lax.rem(x + 1, 4), lax.rem(x + 2, 4)]

    def half(p, xs_, i):
        return ebuf.at[piece_z[p] * 4 + xs_, pl.ds(256 * i, 256), :]

    def own_half(at, i):
        return enc.at[pl.ds(pl.multiple_of(at + 256 * i, 256), 256), :]

    def e_near(i):
        send(own_half(r * 512, i), half(0, x, i), ez_ss.at[0, i], ez_rs.at[0, i], {"head": sibling * 4 + x})

    def e_far(i):
        send(own_half(512 - r * 512, i), half(0, x, i), ez_ss.at[1, i], ez_rs.at[1, i], {"head": opposite * 4 + x})

    def e_step(p, i):
        wait_arrival(half(p, x, i), ez_ss.at[p - 1, i], ez_rs.at[p - 1, i], east)
        if p == 2:
            send(half(2, x, i), half(2, x, i), ez_ss.at[2, i], ez_rs.at[2, i], {"head": sibling * 4 + x})
        x_out(p, i)

    def x_out(p, i):
        for d, where in ((0, east), (1, west)):
            send(half(p, x, i), half(p, x, i), ex_ss.at[p, i, d], ex_rs.at[p, i, d], where)

    def x_relay(p):
        wait_arrival(half(p, xs[1], 0), ex_ss.at[p, 0, 0], ex_rs.at[p, 0, 0], east)
        send(half(p, xs[1], 0), half(p, xs[1], 0), eh_ss.at[p, 0], eh_rs.at[p, 0], east)
        wait_arrival(half(p, xs[2], 1), ex_ss.at[p, 1, 1], ex_rs.at[p, 1, 1], west)
        send(half(p, xs[2], 1), half(p, xs[2], 1), eh_ss.at[p, 1], eh_rs.at[p, 1], west)

    def x_last(p):
        wait_arrival(half(p, xs[1], 1), ex_ss.at[p, 1, 0], ex_rs.at[p, 1, 0], east)
        wait_arrival(half(p, xs[2], 0), ex_ss.at[p, 0, 1], ex_rs.at[p, 0, 1], west)
        wait_arrival(half(p, xs[3], 0), eh_ss.at[p, 0], eh_rs.at[p, 0], east)
        wait_arrival(half(p, xs[3], 1), eh_ss.at[p, 1], eh_rs.at[p, 1], west)

    col_head = lax.broadcasted_iota(jnp.int32, (BEAMS, 256), 1) // HEAD_DIM
    lane = lax.broadcasted_iota(jnp.int32, (8, 128), 1)
    is_top = lax.rem(lane, 8) < 4

    def spread_rows(share):
        halves = []
        for half in range(2):
            scale = jnp.zeros((8, 256), jnp.float32)
            for h in range(4):
                at = 8 * half + h
                scale = jnp.where(
                    col_head[:8] == h, jnp.broadcast_to(share[:, at:at + 1], (8, 256)), scale
                )
            halves.append(scale)
        return jnp.concatenate(halves, axis=0)

    row_of = lax.broadcasted_iota(jnp.int32, (8, 128), 0)

    def swap_rows(tile, step):
        return jnp.where(
            lax.rem(lax.div(row_of, step), 2) == 0, pltpu.roll(tile, 8 - step, 0), pltpu.roll(tile, step, 0)
        )

    def fold(tile):
        turned = swap_rows(swap_rows(pltpu.roll(tile, 4, 0), 2), 1)
        return jnp.sum(pltpu.roll(turned, 0, 1, stride=16, stride_axis=0), axis=0, keepdims=True)

    def unfold(row):
        return pltpu.roll(jnp.broadcast_to(row, (8, 128)), 16, 1, stride=16, stride_axis=0)

    def merge(stats, parts):
        peak = functools.reduce(jnp.maximum, stats)
        factors = [jnp.exp(one - peak) for one in stats]
        sums = functools.reduce(
            lambda a, b: a + b, [f * pltpu.roll(one, 124, 1) for f, one in zip(factors, stats)]
        )
        joined = functools.reduce(
            lambda a, b: a + b, [one * spread_rows(f) for f, one in zip(factors, parts)]
        )
        return peak, sums, joined

    def query_out(t):
        for i in (3, 2, 4, 1, 5, 0, 6):
            m = ring_peers[i]
            if t == 1:
                send(z_own, z_all.at[n], z_ss.at[i], z_rs.at[n], ring(m))
            send(q_own.at[t], q_all.at[t, n], q_ss.at[t, i], q_rs.at[t, n], ring(m))

    def query_swap(t):
        for i, m in enumerate(ring_peers):
            if t == 1:
                wait_arrival(z_all.at[m], z_ss.at[i], z_rs.at[m], ring(m))
            wait_arrival(q_all.at[t, m], q_ss.at[t, i], q_rs.at[t, m], ring(m))
        if t == 1:
            squares = (z_all[0] + z_all[2]) + (z_all[4] + z_all[6])
            zz_own[...] = squares
            zz_all[k] = squares
            send(zz_own, zz_all.at[k], zz_ss.at[0], zz_rs.at[0], partner)
        for g in range(2):
            both_g = (q_all[t, g] + q_all[t, g + 2]) + (q_all[t, g + 4] + q_all[t, g + 6])
            u_all[t, k, g] = both_g
            u_own[t, g] = both_g
        send(u_own.at[t], u_all.at[t, k], u_ss.at[t], u_rs.at[t], partner)

    def query_in(t):
        if t == 1:
            wait_arrival(zz_all.at[other], zz_ss.at[0], zz_rs.at[0], partner)
        wait_arrival(u_all.at[t, other], u_ss.at[t], u_rs.at[t], partner)

    def attend(t, g, scale):
        query = u_all[t, 0, g] + u_all[t, 1, g]
        if scale is not None:
            query = query * scale
        query = query.astype(jnp.bfloat16).astype(jnp.float32)
        spread = jnp.concatenate(
            [jnp.where(col_head == h, query, 0.0) for h in range(4)], axis=0
        ).astype(jnp.bfloat16)
        scores = lax.dot_general(
            spread, kv[2 * g], (((1,), (1,)), ((), ())), preferred_element_type=jnp.float32
        ) * 0.125
        top = jnp.max(scores, axis=-1, keepdims=True)
        expo = jnp.exp(scores - top)
        total = jnp.sum(expo, axis=-1, keepdims=True)
        mixed = jnp.dot(expo.astype(jnp.bfloat16), kv[2 * g + 1], preferred_element_type=jnp.float32)
        ctx = jnp.zeros((BEAMS, 256), jnp.float32)
        stats = jnp.zeros((8, 128), jnp.float32)
        for h in range(4):
            ctx += jnp.where(col_head == h, mixed[16 * h:16 * h + 16], 0.0)
            for half in range(2):
                at = 16 * h + 8 * half
                stats = jnp.where(lane == 8 * half + h, top[at:at + 8], stats)
                stats = jnp.where(lane == 8 * half + 4 + h, total[at:at + 8], stats)
        return ctx.astype(jnp.bfloat16), stats

    z_on(0, 0)
    z_on(0, 1)
    e_near(0)
    e_far(0)
    e_near(1)
    e_far(1)
    x_out(0, 0)
    x_out(0, 1)
    send(shard_both(k), shard_both(k), wc_ss.at[0, 0], wc_rs.at[0, 0], partner)

    for i in range(BEAMS):
        picked[pl.ds(i, 1), :] = first[pl.ds(parents[0, i], 1), :]
    start = picked[...] + tokens[0].astype(jnp.float32)
    pre[...] = start
    mean = jnp.sum(start * start, axis=-1, keepdims=True) * (1.0 / 4096.0)
    picked[...] = start * lax.rsqrt(mean + 1e-06) * gain[...]
    q_own[0] = jnp.dot(picked[:, feats].astype(jnp.bfloat16), wq[...], preferred_element_type=jnp.float32)
    q_all[0, n] = q_own[0]
    query_out(0)

    z_step(1, 0)
    z_step(2, 0)
    z_step(1, 1)
    z_step(2, 1)
    x_relay(0)
    e_step(1, 0)
    e_step(1, 1)
    z_step(3, 0)
    z_step(4, 0)
    z_step(3, 1)
    z_step(4, 1)
    e_step(2, 0)
    e_step(2, 1)
    y_relay(1)
    y_relay(2)
    x_relay(1)
    z_step(5, 0)
    z_step(6, 0)
    z_step(5, 1)
    z_step(6, 1)
    x_last(0)
    y_relay(3)
    y_relay(4)
    y_cross(1)
    y_cross(2)
    x_relay(2)
    x_last(1)
    e_step(3, 0)
    e_step(3, 1)
    z_step(7, 0)
    z_step(7, 1)
    y_last(1)
    y_last(2)
    query_swap(0)
    y_relay(5)
    y_relay(6)
    y_cross(3)
    y_cross(4)
    x_relay(3)
    y_last(3)
    y_last(4)
    x_last(2)
    y_relay(7)
    y_cross(5)
    y_cross(6)
    y_last(5)
    y_last(6)
    x_last(3)
    y_cross(7)
    y_last(7)

    @pl.loop(0, 8)
    def _(i):
        at = pl.ds(pl.multiple_of(i * 64, 64), 64)
        acc = jnp.zeros((64, 128), jnp.float32)
        for f in range(HEAD):
            block = ebuf[f, at, :].astype(jnp.float32)
            block = block * block
            acc += block[:, :128] + block[:, 128:]
        scale = lax.rsqrt(jnp.sum(acc, axis=-1, keepdims=True) * (1.0 / 4096.0) + 1e-06)
        for f in range(HEAD):
            cols = slice(256 * f, 256 * f + 256)
            block = ebuf[f, at, :].astype(jnp.float32) * scale * enc_gain[:, cols]
            nbuf[at, cols] = block.astype(jnp.bfloat16)

    wait_arrival(shard_both(other), wc_ss.at[0, 0], wc_rs.at[0, 0], partner)
    for q in range(1, 8):
        for j in range(4):
            wait_arrival(both(q, j, other), wc_ss.at[q, j], wc_rs.at[q, j], partner)

    @pl.loop(0, 4)
    def _(i):
        kv[i] = jnp.dot(nbuf[...], wbuf[i], preferred_element_type=jnp.float32).astype(jnp.bfloat16)

    for t in range(STEPS):
        scale = None
        if t == 1:
            for j in range(4):
                part[:, 128 * j:128 * j + 128] = l_all[:, j, :]
            part[...] = part[...] + pre[:, feats]
            for i in range(BEAMS):
                local_rows[pl.ds(i, 1), :] = part[pl.ds(parents[1, i], 1), :]
            rows = local_rows[...] + tokens[1, :, feats].astype(jnp.float32)
            squares = jnp.sum(rows * rows, axis=-1, keepdims=True)
            z_own[...] = fold(
                jnp.where(lane == 0, squares[:8], jnp.where(lane == 1, squares[8:], 0.0))
            )
            z_all[n] = z_own[...]
            scaled = rows * gain[:, feats]
            high = scaled.astype(jnp.bfloat16)
            low = (scaled - high.astype(jnp.float32)).astype(jnp.bfloat16)
            q_own[1] = jnp.dot(high, wq[...], preferred_element_type=jnp.float32) + jnp.dot(
                low, wq[...], preferred_element_type=jnp.float32
            )
            q_all[1, n] = q_own[1]
            query_out(1)
            query_swap(1)
            for i, p in enumerate(seq_peers):
                wait_arrival(f_all.at[0, p], f_ss.at[0, i], f_rs.at[0, p], {"seq": p})
            for i, p in enumerate(head_peers):
                send(f_all.at[0], g_all.at[0, c], g_ss.at[0, i], g_rs.at[0, c], {"head": p})
            g_all[0, c] = f_all[0]
        query_in(t)
        if t == 1:
            table = lax.rsqrt(unfold(zz_all[0] + zz_all[1]) * (1.0 / 4096.0) + 1e-06)
            scale = jnp.concatenate([table[:, :1], table[:, 1:2]], axis=0)
        for slot, g, order in ((1, r, (3, 1, 5)), (0, 1 - r, (2, 4, 0, 6))):
            ctx, stats = attend(t, g, scale)
            c_own[t, slot] = ctx
            t_own[t, slot] = fold(stats)
            for i in order:
                m = ring_peers[i]
                send(t_own.at[t, slot], t_all.at[t, n], t_ss.at[t, i], t_rs.at[t, n], ring(m))
                send(c_own.at[t, slot], c_all.at[t, n], c_ss.at[t, i], c_rs.at[t, n], ring(m))
        c_all[t, n] = c_own[t, 1]
        t_all[t, n] = t_own[t, 1]
        if t == 1:
            for i, p in enumerate(head_peers):
                wait_arrival(g_all.at[0, p], g_ss.at[0, i], g_rs.at[0, p], {"head": p})
            for i in range(8):
                for j in range(4):
                    cols = slice(512 * i + 128 * j, 512 * i + 128 * j + 128)
                    one_col = g_all[0, :, i, j, :]
                    out_first[:, cols] = one_col
                    full[:, cols] = pre[:, cols] + one_col
            for i in range(BEAMS):
                picked[pl.ds(i, 1), :] = full[pl.ds(parents[1, i], 1), :]
            out_pre[...] = picked[...] + tokens[1].astype(jnp.float32)
        for i, m in enumerate(ring_peers):
            wait_arrival(t_all.at[t, m], t_ss.at[t, i], t_rs.at[t, m], ring(m))
            wait_arrival(c_all.at[t, m], c_ss.at[t, i], c_rs.at[t, m], ring(m))
        peak, sums, joined = merge(
            [unfold(t_all[t, i]) for i in range(8)], [c_all[t, i].astype(jnp.float32) for i in range(8)]
        )
        stats = jnp.where(is_top, peak, pltpu.roll(sums, 4, 1))
        v_own[t] = joined
        m_own[t] = stats
        v_all[t, k] = joined
        m_all[t, k] = stats
        send(m_own.at[t], m_all.at[t, k], m_ss.at[t], m_rs.at[t], partner)
        send(v_own.at[t], v_all.at[t, k], v_ss.at[t], v_rs.at[t], partner)
        wait_arrival(m_all.at[t, other], m_ss.at[t], m_rs.at[t], partner)
        wait_arrival(v_all.at[t, other], v_ss.at[t], v_rs.at[t], partner)
        peak, sums, joined = merge([m_all[t, 0], m_all[t, 1]], [v_all[t, 0], v_all[t, 1]])
        context = (joined / spread_rows(sums)).astype(jnp.bfloat16)
        partial = jnp.dot(context, wo[...], preferred_element_type=jnp.float32)
        for j in range(4):
            p_own[t, :, j, :] = partial[:, 128 * j:128 * j + 128]
        p_all[t, c] = p_own[t, c]
        for i, p in enumerate(head_peers):
            send(p_own.at[t, p], p_all.at[t, c], p_ss.at[t, i], p_rs.at[t, c], {"head": p})
        for i, p in enumerate(head_peers):
            wait_arrival(p_all.at[t, p], p_ss.at[t, i], p_rs.at[t, p], {"head": p})
        row = p_all[t, 0]
        for i in range(1, HEAD):
            row += p_all[t, i]
        f_own[t] = row
        f_all[t, s] = row
        if t == 0:
            for i, p in enumerate(head_peers):
                send(f_own.at[t], l_all.at[c], l_ss.at[i], l_rs.at[c], {"head": p})
            l_all[c] = row
        for i, p in enumerate(seq_peers):
            send(f_own.at[t], f_all.at[t, s], f_ss.at[t, i], f_rs.at[t, s], {"seq": p})
        if t == 0:
            for i, p in enumerate(head_peers):
                wait_arrival(l_all.at[p], l_ss.at[i], l_rs.at[p], {"head": p})
    for i, p in enumerate(seq_peers):
        wait_arrival(f_all.at[1, p], f_ss.at[1, i], f_rs.at[1, p], {"seq": p})
    for i, p in enumerate(head_peers):
        send(f_all.at[1], g_all.at[1, c], g_ss.at[1, i], g_rs.at[1, c], {"head": p})
    g_all[1, c] = f_all[1]
    for i, p in enumerate(head_peers):
        wait_arrival(g_all.at[1, p], g_ss.at[1, i], g_rs.at[1, p], {"head": p})
    for i in range(8):
        for j in range(4):
            cols = slice(512 * i + 128 * j, 512 * i + 128 * j + 128)
            one_col = g_all[1, :, i, j, :]
            out_second[:, cols] = one_col
    for copy in sent:
        copy.wait_send()


def on_device(
    enc_out, enc_gain, key_weight, value_weight, query_weight, out_weight,
    dec_gain, beam_state, parents, token_embed,
):
    vmem = pl.BlockSpec(memory_space=pltpu.VMEM)
    f32, bf16 = jnp.float32, jnp.bfloat16
    dma = pltpu.SemaphoreType.DMA
    rows = jax.ShapeDtypeStruct((BEAMS, 4096), f32)

    def pair(*shape):
        return [dma(shape), dma(shape)]

    before, once, twice = pl.pallas_call(
        kernel,
        out_shape=(rows, rows, rows),
        in_specs=[vmem] * 8 + [pl.BlockSpec(memory_space=pltpu.SMEM), vmem],
        out_specs=(vmem, vmem, vmem),
        scratch_shapes=[
            pltpu.VMEM((HEAD, 512, 256), bf16),
            pltpu.VMEM((512, 4096), bf16),
            pltpu.VMEM((4, 4096, 256), bf16),
            pltpu.VMEM((4, 512, 256), bf16),
            pltpu.VMEM((BEAMS, 4096), f32),
            pltpu.VMEM((BEAMS, 512), f32),
            pltpu.VMEM((BEAMS, 4096), f32),
            pltpu.VMEM((BEAMS, 512), f32),
            pltpu.VMEM((BEAMS, 4096), f32),
            pltpu.VMEM((STEPS, BEAMS, 256), f32),
            pltpu.VMEM((STEPS, 8, BEAMS, 256), f32),
            pltpu.VMEM((STEPS, 2, BEAMS, 256), f32),
            pltpu.VMEM((STEPS, 2, 2, BEAMS, 256), f32),
            pltpu.VMEM((1, 128), f32),
            pltpu.VMEM((8, 1, 128), f32),
            pltpu.VMEM((1, 128), f32),
            pltpu.VMEM((2, 1, 128), f32),
            pltpu.VMEM((STEPS, 2, BEAMS, 256), bf16),
            pltpu.VMEM((STEPS, 8, BEAMS, 256), bf16),
            pltpu.VMEM((STEPS, 2, 1, 128), f32),
            pltpu.VMEM((STEPS, 8, 1, 128), f32),
            pltpu.VMEM((STEPS, 8, 128), f32),
            pltpu.VMEM((STEPS, 2, 8, 128), f32),
            pltpu.VMEM((STEPS, BEAMS, 256), f32),
            pltpu.VMEM((STEPS, 2, BEAMS, 256), f32),
            pltpu.VMEM((STEPS, BEAMS, 4, 128), f32),
            pltpu.VMEM((STEPS, HEAD, 4, 128), f32),
            pltpu.VMEM((STEPS, 4, 128), f32),
            pltpu.VMEM((STEPS, SEQ, 4, 128), f32),
            pltpu.VMEM((BEAMS, 4, 128), f32),
            pltpu.VMEM((STEPS, BEAMS, 8, 4, 128), f32),
            dma((3,)),
            *pair(8, 2), *pair(8, 2, 2), *pair(8, 2), *pair(8, 4), *pair(3, 2), *pair(4, 2, 2), *pair(4, 2),
            *pair(STEPS, 8), *pair(STEPS), *pair(8), *pair(1), *pair(STEPS, 8), *pair(STEPS, 8),
            *pair(STEPS), *pair(STEPS), *pair(STEPS, HEAD), *pair(STEPS, SEQ), *pair(HEAD), *pair(STEPS, HEAD),
        ],
        compiler_params=pltpu.CompilerParams(collective_id=1, has_side_effects=True),
        name="beam_decode",
    )(
        enc_out, enc_gain.reshape(1, 4096), key_weight, value_weight, query_weight, out_weight,
        dec_gain.reshape(1, 4096), beam_state, parents, token_embed,
    )
    return before + twice, once + twice


def solution(mesh):
    placed = (
        P(("src", "seq"), "head"),
        P(),
        P("seq", "head"),
        P("seq", "head"),
        P("seq", "head"),
        P("head", "seq"),
        P(),
        P("src", None),
        P("src", None),
        P("src", None, None),
    )
    return jax.shard_map(
        on_device,
        mesh=mesh,
        in_specs=placed,
        out_specs=(P("src", None), P("src", None)),
        check_vma=False,
    )
```

```python
import functools

import jax
import jax.numpy as jnp
from jax import lax
from jax.experimental import pallas as pl
from jax.experimental.pallas import tpu as pltpu
from jax.sharding import PartitionSpec as P

MESH = pl.DeviceIdType.MESH
HEAD_DIM = 64
BEAMS = 16
STEPS = 2
SEQ = 8
HEAD = 16


def place():
    y = lax.axis_index("src")
    s = lax.axis_index("seq")
    c = lax.axis_index("head")
    zh, k = lax.div(s, 2), lax.rem(s, 2)
    zl, x = lax.div(c, 4), lax.rem(c, 4)
    b, r = lax.rem(zl, 2), lax.div(zl, 2)
    return y, s, c, k, zl, x, b, r, zh * 2 + r


def node_id(m, k, b, x):
    return {"seq": lax.div(m, 2) * 2 + k, "head": (lax.rem(m, 2) * 2 + b) * 4 + x}


def partner_id(s, k):
    return {"seq": s + 1 - 2 * k}


def start_send(sent, src, dst, ss, rs, where):
    copy = pltpu.make_async_remote_copy(
        src_ref=src, dst_ref=dst, send_sem=ss, recv_sem=rs, device_id=where, device_id_type=MESH,
    )
    copy.start()
    sent.append(copy)


def wait_arrival(dst, ss, rs, where):
    pltpu.make_async_remote_copy(
        src_ref=dst, dst_ref=dst, send_sem=ss, recv_sem=rs, device_id=where, device_id_type=MESH,
    ).wait_recv()


OFFSETS = (0, -1, 1, -2, 2, -3, 3, 4)
BY_OFFSET = {off: q for q, off in enumerate(OFFSETS)}


def kernel(
    enc, enc_gain_in, wk, wv, wq_in, wo_in, gain_in, first_in, parents, tokens_in,
    pre_out, first_out, second_out,
    enc_gain, wq, wo, gain, first, tokens, out_pre, out_first, out_second,
    ebuf, nbuf, wbuf, kv,
    pre, part, picked, local_rows, full,
    q_own, q_all, u_own, u_all, z_own, z_all, zz_own, zz_all, c_own, c_all, t_own, t_all, m_own, m_all, v_own, v_all,
    p_own, p_all, f_own, f_all, l_all, g_all,
    own_sem, in_sem, out_sem, wz_ss, wz_rs, wy_ss, wy_rs, wh_ss, wh_rs, wc_ss, wc_rs, ez_ss, ez_rs, ex_ss, ex_rs, eh_ss, eh_rs,
    q_ss, q_rs, u_ss, u_rs, z_ss, z_rs, zz_ss, zz_rs, c_ss, c_rs, t_ss, t_rs, m_ss, m_rs, v_ss, v_rs,
    p_ss, p_rs, f_ss, f_rs, l_ss, l_rs, g_ss, g_rs,
):
    y, s, c, k, zl, x, b, r, n = place()
    up, down = {"src": lax.rem(y + 1, 4)}, {"src": lax.rem(y + 3, 4)}
    east = {"head": zl * 4 + lax.rem(x + 1, 4)}
    west = {"head": zl * 4 + lax.rem(x + 3, 4)}
    partner = partner_id(s, k)
    right = node_id(lax.rem(n + 1, 8), k, b, x)
    left = node_id(lax.rem(n + 7, 8), k, b, x)
    sibling = zl + 1 - 2 * b
    opposite = lax.rem(zl + 2, 4)
    quarters = [y, lax.rem(y + 3, 4), lax.rem(y + 1, 4), lax.rem(y + 2, 4)]

    def rows_of(m, quarter, core):
        return pl.ds(pl.multiple_of((lax.div(m, 2) * 2 + core) * 512 + quarter * 128, 128), 128)

    def nodes(q):
        return lax.rem(n + 8 + OFFSETS[q], 8)

    def both(q, j, core):
        m = nodes(q)
        return wbuf.at[pl.ds(2 * lax.rem(m, 2), 2), rows_of(m, quarters[j], core), :]

    def one(q, j, mat):
        m = nodes(q)
        return wbuf.at[2 * lax.rem(m, 2) + mat, rows_of(m, quarters[j], k), :]

    def shard(mat):
        at = pl.ds(pl.multiple_of(s * 512, 512), 512)
        return wbuf.at[2 * r + mat, at, :]

    def shard_both(core):
        at = pl.ds(pl.multiple_of((lax.div(n, 2) * 2 + core) * 512, 512), 512)
        return wbuf.at[pl.ds(2 * r, 2), at, :]

    def local(src, dst, i):
        copy = pltpu.make_async_copy(src, dst, own_sem.at[i])
        copy.start()
        return copy

    near = pl.ds(pl.multiple_of(r * 512, 512), 512)
    far = pl.ds(pl.multiple_of(512 - r * 512, 512), 512)
    seq_peers = [lax.rem(s + i, SEQ) for i in range(1, SEQ)]
    head_peers = [lax.rem(c + i, HEAD) for i in range(1, HEAD)]
    ring_peers = [lax.rem(n + i, 8) for i in range(1, 8)]
    other = 1 - k
    feats = pl.ds(pl.multiple_of(s * 512, 512), 512)

    def ring(m):
        return node_id(m, k, b, x)

    barrier = pltpu.get_barrier_semaphore()
    greet = [up, down, east, west, partner, right, left]
    greet += [{"head": sibling * 4 + x}, {"head": opposite * 4 + x}]
    for where in greet:
        pl.semaphore_signal(barrier, inc=1, device_id=where, device_id_type=MESH)
    locals_ = [
        local(wk, shard(0), 0),
        local(wv, shard(1), 1),
        local(enc.at[near, :], ebuf.at[c], 2),
    ]
    loads = [
        pltpu.make_async_copy(src, dst, in_sem.at[i])
        for i, (src, dst) in enumerate(
            (
                (first_in, first), (tokens_in, tokens), (gain_in, gain), (wq_in, wq),
                (enc_gain_in, enc_gain), (wo_in, wo),
            )
        )
    ]
    for copy in loads:
        copy.start()
    for copy in locals_:
        copy.wait()
    pl.semaphore_wait(barrier, len(greet))

    sent = []
    send = functools.partial(start_send, sent)

    def z_on(q, mat):
        off = OFFSETS[q]
        if -3 < off <= 0 or (off == -3 and mat == 0):
            t = 7 if off == -3 else BY_OFFSET[off - 1]
            send(one(q, 0, mat), one(q, 0, mat), wz_ss.at[t, mat], wz_rs.at[t, mat], right)
        if 0 <= off < 3 or (off == 3 and mat == 1):
            t = 7 if off == 3 else BY_OFFSET[off + 1]
            send(one(q, 0, mat), one(q, 0, mat), wz_ss.at[t, mat], wz_rs.at[t, mat], left)

    def z_step(q, mat):
        wait_arrival(one(q, 0, mat), wz_ss.at[q, mat], wz_rs.at[q, mat], right)
        z_on(q, mat)
        send(one(q, 0, mat), one(q, 0, mat), wy_ss.at[q, mat, 0], wy_rs.at[q, mat, 0], up)
        send(one(q, 0, mat), one(q, 0, mat), wy_ss.at[q, mat, 1], wy_rs.at[q, mat, 1], down)
        if mat == 1:
            cross(q, 0)

    def cross(q, j):
        send(both(q, j, k), both(q, j, k), wc_ss.at[q, j], wc_rs.at[q, j], partner)

    def y_relay(q):
        wait_arrival(one(q, 1, 0), wy_ss.at[q, 0, 0], wy_rs.at[q, 0, 0], up)
        send(one(q, 1, 0), one(q, 1, 0), wh_ss.at[q, 0], wh_rs.at[q, 0], up)
        wait_arrival(one(q, 2, 1), wy_ss.at[q, 1, 1], wy_rs.at[q, 1, 1], down)
        send(one(q, 2, 1), one(q, 2, 1), wh_ss.at[q, 1], wh_rs.at[q, 1], down)

    def y_cross(q):
        wait_arrival(one(q, 1, 1), wy_ss.at[q, 1, 0], wy_rs.at[q, 1, 0], up)
        cross(q, 1)
        wait_arrival(one(q, 2, 0), wy_ss.at[q, 0, 1], wy_rs.at[q, 0, 1], down)
        cross(q, 2)

    def y_last(q):
        wait_arrival(one(q, 3, 0), wh_ss.at[q, 0], wh_rs.at[q, 0], up)
        wait_arrival(one(q, 3, 1), wh_ss.at[q, 1], wh_rs.at[q, 1], down)
        cross(q, 3)

    piece_z = [zl, sibling, opposite, lax.rem(sibling + 2, 4)]
    xs = [x, lax.rem(x + 3, 4), lax.rem(x + 1, 4), lax.rem(x + 2, 4)]

    def half(p, xs_, i):
        return ebuf.at[piece_z[p] * 4 + xs_, pl.ds(256 * i, 256), :]

    def own_half(at, i):
        return enc.at[pl.ds(pl.multiple_of(at + 256 * i, 256), 256), :]

    def e_near(i):
        send(half(0, x, i), half(0, x, i), ez_ss.at[0, i], ez_rs.at[0, i], {"head": sibling * 4 + x})

    def e_far(i):
        send(own_half(512 - r * 512, i), half(0, x, i), ez_ss.at[1, i], ez_rs.at[1, i], {"head": opposite * 4 + x})

    def e_step(p, i):
        wait_arrival(half(p, x, i), ez_ss.at[p - 1, i], ez_rs.at[p - 1, i], east)
        if p == 2:
            send(half(2, x, i), half(2, x, i), ez_ss.at[2, i], ez_rs.at[2, i], {"head": sibling * 4 + x})
        x_out(p, i)

    def x_out(p, i):
        for d, where in ((0, east), (1, west)):
            send(half(p, x, i), half(p, x, i), ex_ss.at[p, i, d], ex_rs.at[p, i, d], where)

    def x_relay(p):
        wait_arrival(half(p, xs[1], 0), ex_ss.at[p, 0, 0], ex_rs.at[p, 0, 0], east)
        send(half(p, xs[1], 0), half(p, xs[1], 0), eh_ss.at[p, 0], eh_rs.at[p, 0], east)
        wait_arrival(half(p, xs[2], 1), ex_ss.at[p, 1, 1], ex_rs.at[p, 1, 1], west)
        send(half(p, xs[2], 1), half(p, xs[2], 1), eh_ss.at[p, 1], eh_rs.at[p, 1], west)

    def x_last(p):
        wait_arrival(half(p, xs[1], 1), ex_ss.at[p, 1, 0], ex_rs.at[p, 1, 0], east)
        wait_arrival(half(p, xs[2], 0), ex_ss.at[p, 0, 1], ex_rs.at[p, 0, 1], west)
        wait_arrival(half(p, xs[3], 0), eh_ss.at[p, 0], eh_rs.at[p, 0], east)
        wait_arrival(half(p, xs[3], 1), eh_ss.at[p, 1], eh_rs.at[p, 1], west)

    col_head = lax.broadcasted_iota(jnp.int32, (BEAMS, 256), 1) // HEAD_DIM
    lane = lax.broadcasted_iota(jnp.int32, (8, 128), 1)
    is_top = lax.rem(lane, 8) < 4

    def spread_rows(share):
        halves = []
        for half in range(2):
            scale = jnp.zeros((8, 256), jnp.float32)
            for h in range(4):
                at = 8 * half + h
                scale = jnp.where(
                    col_head[:8] == h, jnp.broadcast_to(share[:, at:at + 1], (8, 256)), scale
                )
            halves.append(scale)
        return jnp.concatenate(halves, axis=0)

    row_of = lax.broadcasted_iota(jnp.int32, (8, 128), 0)

    def swap_rows(tile, step):
        return jnp.where(
            lax.rem(lax.div(row_of, step), 2) == 0, pltpu.roll(tile, 8 - step, 0), pltpu.roll(tile, step, 0)
        )

    def fold(tile):
        turned = swap_rows(swap_rows(pltpu.roll(tile, 4, 0), 2), 1)
        return jnp.sum(pltpu.roll(turned, 0, 1, stride=16, stride_axis=0), axis=0, keepdims=True)

    def unfold(row):
        return pltpu.roll(jnp.broadcast_to(row, (8, 128)), 16, 1, stride=16, stride_axis=0)

    def merge(stats, parts):
        peak = functools.reduce(jnp.maximum, stats)
        factors = [jnp.exp(one - peak) for one in stats]
        sums = functools.reduce(
            lambda a, b: a + b, [f * pltpu.roll(one, 124, 1) for f, one in zip(factors, stats)]
        )
        joined = functools.reduce(
            lambda a, b: a + b, [one * spread_rows(f) for f, one in zip(factors, parts)]
        )
        return peak, sums, joined

    def query_out(t):
        for i in (3, 2, 4, 1, 5, 0, 6):
            m = ring_peers[i]
            if t == 1:
                send(z_own, z_all.at[n], z_ss.at[i], z_rs.at[n], ring(m))
            send(q_own.at[t], q_all.at[t, n], q_ss.at[t, i], q_rs.at[t, n], ring(m))

    def query_swap(t):
        for i, m in enumerate(ring_peers):
            if t == 1:
                wait_arrival(z_all.at[m], z_ss.at[i], z_rs.at[m], ring(m))
            wait_arrival(q_all.at[t, m], q_ss.at[t, i], q_rs.at[t, m], ring(m))
        if t == 1:
            squares = (z_all[0] + z_all[2]) + (z_all[4] + z_all[6])
            zz_own[...] = squares
            zz_all[k] = squares
            send(zz_own, zz_all.at[k], zz_ss.at[0], zz_rs.at[0], partner)
        for g in range(2):
            both_g = (q_all[t, g] + q_all[t, g + 2]) + (q_all[t, g + 4] + q_all[t, g + 6])
            u_all[t, k, g] = both_g
            u_own[t, g] = both_g
        send(u_own.at[t], u_all.at[t, k], u_ss.at[t], u_rs.at[t], partner)

    def query_in(t):
        if t == 1:
            wait_arrival(zz_all.at[other], zz_ss.at[0], zz_rs.at[0], partner)
        wait_arrival(u_all.at[t, other], u_ss.at[t], u_rs.at[t], partner)

    def attend(t, g, scale):
        query = u_all[t, 0, g] + u_all[t, 1, g]
        if scale is not None:
            query = query * scale
        query = query.astype(jnp.bfloat16).astype(jnp.float32)
        spread = jnp.concatenate(
            [jnp.where(col_head == h, query, 0.0) for h in range(4)], axis=0
        ).astype(jnp.bfloat16)
        scores = lax.dot_general(
            spread, kv[2 * g], (((1,), (1,)), ((), ())), preferred_element_type=jnp.float32
        ) * 0.125
        top = jnp.max(scores, axis=-1, keepdims=True)
        expo = jnp.exp(scores - top)
        total = jnp.sum(expo, axis=-1, keepdims=True)
        mixed = jnp.dot(expo.astype(jnp.bfloat16), kv[2 * g + 1], preferred_element_type=jnp.float32)
        ctx = jnp.zeros((BEAMS, 256), jnp.float32)
        stats = jnp.zeros((8, 128), jnp.float32)
        for h in range(4):
            ctx += jnp.where(col_head == h, mixed[16 * h:16 * h + 16], 0.0)
            for half in range(2):
                at = 16 * h + 8 * half
                stats = jnp.where(lane == 8 * half + h, top[at:at + 8], stats)
                stats = jnp.where(lane == 8 * half + 4 + h, total[at:at + 8], stats)
        return ctx.astype(jnp.bfloat16), stats

    z_on(0, 0)
    z_on(0, 1)
    e_near(0)
    e_far(0)
    e_near(1)
    e_far(1)
    x_out(0, 0)
    x_out(0, 1)
    send(shard_both(k), shard_both(k), wc_ss.at[0, 0], wc_rs.at[0, 0], partner)

    for copy in loads:
        copy.wait()
    for i in range(BEAMS):
        picked[pl.ds(i, 1), :] = first[pl.ds(parents[0, i], 1), :]
    start = picked[...] + tokens[0].astype(jnp.float32)
    pre[...] = start
    mean = jnp.sum(start * start, axis=-1, keepdims=True) * (1.0 / 4096.0)
    picked[...] = start * lax.rsqrt(mean + 1e-06) * gain[...]
    q_own[0] = jnp.dot(picked[:, feats].astype(jnp.bfloat16), wq[...], preferred_element_type=jnp.float32)
    q_all[0, n] = q_own[0]

    z_step(1, 0)
    z_step(2, 0)
    z_step(1, 1)
    z_step(2, 1)
    x_relay(0)
    e_step(1, 0)
    e_step(1, 1)
    z_step(3, 0)
    z_step(4, 0)
    z_step(3, 1)
    z_step(4, 1)
    e_step(2, 0)
    e_step(2, 1)
    y_relay(1)
    y_relay(2)
    x_relay(1)
    z_step(5, 0)
    z_step(6, 0)
    z_step(5, 1)
    z_step(6, 1)
    x_last(0)
    y_relay(3)
    y_relay(4)
    y_cross(1)
    y_cross(2)
    x_relay(2)
    x_last(1)
    e_step(3, 0)
    e_step(3, 1)
    z_step(7, 0)
    z_step(7, 1)
    query_out(0)
    y_last(1)
    y_last(2)
    query_swap(0)
    y_relay(5)
    y_relay(6)
    y_cross(3)
    y_cross(4)
    x_relay(3)
    y_last(3)
    y_last(4)
    x_last(2)
    y_relay(7)
    y_cross(5)
    y_cross(6)
    y_last(5)
    y_last(6)
    x_last(3)
    y_cross(7)
    y_last(7)

    @pl.loop(0, 8)
    def _(i):
        at = pl.ds(pl.multiple_of(i * 64, 64), 64)
        acc = jnp.zeros((64, 128), jnp.float32)
        for f in range(HEAD):
            block = ebuf[f, at, :].astype(jnp.float32)
            block = block * block
            acc += block[:, :128] + block[:, 128:]
        scale = lax.rsqrt(jnp.sum(acc, axis=-1, keepdims=True) * (1.0 / 4096.0) + 1e-06)
        for f in range(HEAD):
            cols = slice(256 * f, 256 * f + 256)
            block = ebuf[f, at, :].astype(jnp.float32) * scale * enc_gain[:, cols]
            nbuf[at, cols] = block.astype(jnp.bfloat16)

    wait_arrival(shard_both(other), wc_ss.at[0, 0], wc_rs.at[0, 0], partner)
    for q in range(1, 8):
        for j in range(4):
            wait_arrival(both(q, j, other), wc_ss.at[q, j], wc_rs.at[q, j], partner)

    @pl.loop(0, 4)
    def _(i):
        kv[i] = jnp.dot(nbuf[...], wbuf[i], preferred_element_type=jnp.float32).astype(jnp.bfloat16)

    for t in range(STEPS):
        scale = None
        if t == 1:
            for j in range(4):
                part[:, 128 * j:128 * j + 128] = l_all[:, j, :]
            part[...] = part[...] + pre[:, feats]
            for i in range(BEAMS):
                local_rows[pl.ds(i, 1), :] = part[pl.ds(parents[1, i], 1), :]
            rows = local_rows[...] + tokens[1, :, feats].astype(jnp.float32)
            squares = jnp.sum(rows * rows, axis=-1, keepdims=True)
            z_own[...] = fold(
                jnp.where(lane == 0, squares[:8], jnp.where(lane == 1, squares[8:], 0.0))
            )
            z_all[n] = z_own[...]
            scaled = rows * gain[:, feats]
            high = scaled.astype(jnp.bfloat16)
            low = (scaled - high.astype(jnp.float32)).astype(jnp.bfloat16)
            q_own[1] = jnp.dot(high, wq[...], preferred_element_type=jnp.float32) + jnp.dot(
                low, wq[...], preferred_element_type=jnp.float32
            )
            q_all[1, n] = q_own[1]
            query_out(1)
            query_swap(1)
            for i, p in enumerate(seq_peers):
                wait_arrival(f_all.at[0, p], f_ss.at[0, i], f_rs.at[0, p], {"seq": p})
            for i, p in enumerate(head_peers):
                send(f_all.at[0], g_all.at[0, c], g_ss.at[0, i], g_rs.at[0, c], {"head": p})
            g_all[0, c] = f_all[0]
        query_in(t)
        if t == 1:
            table = lax.rsqrt(unfold(zz_all[0] + zz_all[1]) * (1.0 / 4096.0) + 1e-06)
            scale = jnp.concatenate([table[:, :1], table[:, 1:2]], axis=0)
        for slot, g, order in ((1, r, (3, 1, 5)), (0, 1 - r, (2, 4, 0, 6))):
            ctx, stats = attend(t, g, scale)
            c_own[t, slot] = ctx
            t_own[t, slot] = fold(stats)
            for i in order:
                m = ring_peers[i]
                send(t_own.at[t, slot], t_all.at[t, n], t_ss.at[t, i], t_rs.at[t, n], ring(m))
                send(c_own.at[t, slot], c_all.at[t, n], c_ss.at[t, i], c_rs.at[t, n], ring(m))
        c_all[t, n] = c_own[t, 1]
        t_all[t, n] = t_own[t, 1]
        if t == 1:
            for i, p in enumerate(head_peers):
                wait_arrival(g_all.at[0, p], g_ss.at[0, i], g_rs.at[0, p], {"head": p})
            for i in range(8):
                for j in range(4):
                    cols = slice(512 * i + 128 * j, 512 * i + 128 * j + 128)
                    one_col = g_all[0, :, i, j, :]
                    out_first[:, cols] = one_col
                    full[:, cols] = pre[:, cols] + one_col
            for i in range(BEAMS):
                picked[pl.ds(i, 1), :] = full[pl.ds(parents[1, i], 1), :]
            out_pre[...] = picked[...] + tokens[1].astype(jnp.float32)
            stores = [
                pltpu.make_async_copy(out_pre, pre_out, out_sem.at[0]),
                pltpu.make_async_copy(out_first, first_out, out_sem.at[1]),
            ]
            for copy in stores:
                copy.start()
        for i, m in enumerate(ring_peers):
            wait_arrival(t_all.at[t, m], t_ss.at[t, i], t_rs.at[t, m], ring(m))
            wait_arrival(c_all.at[t, m], c_ss.at[t, i], c_rs.at[t, m], ring(m))
        peak, sums, joined = merge(
            [unfold(t_all[t, i]) for i in range(8)], [c_all[t, i].astype(jnp.float32) for i in range(8)]
        )
        stats = jnp.where(is_top, peak, pltpu.roll(sums, 4, 1))
        v_own[t] = joined
        m_own[t] = stats
        v_all[t, k] = joined
        m_all[t, k] = stats
        send(m_own.at[t], m_all.at[t, k], m_ss.at[t], m_rs.at[t], partner)
        send(v_own.at[t], v_all.at[t, k], v_ss.at[t], v_rs.at[t], partner)
        wait_arrival(m_all.at[t, other], m_ss.at[t], m_rs.at[t], partner)
        wait_arrival(v_all.at[t, other], v_ss.at[t], v_rs.at[t], partner)
        peak, sums, joined = merge([m_all[t, 0], m_all[t, 1]], [v_all[t, 0], v_all[t, 1]])
        context = (joined / spread_rows(sums)).astype(jnp.bfloat16)
        partial = jnp.dot(context, wo[...], preferred_element_type=jnp.float32)
        for j in range(4):
            p_own[t, :, j, :] = partial[:, 128 * j:128 * j + 128]
        p_all[t, c] = p_own[t, c]
        for i, p in enumerate(head_peers):
            send(p_own.at[t, p], p_all.at[t, c], p_ss.at[t, i], p_rs.at[t, c], {"head": p})
        for i, p in enumerate(head_peers):
            wait_arrival(p_all.at[t, p], p_ss.at[t, i], p_rs.at[t, p], {"head": p})
        row = p_all[t, 0]
        for i in range(1, HEAD):
            row += p_all[t, i]
        f_own[t] = row
        f_all[t, s] = row
        if t == 0:
            for i, p in enumerate(head_peers):
                send(f_own.at[t], l_all.at[c], l_ss.at[i], l_rs.at[c], {"head": p})
            l_all[c] = row
        for i, p in enumerate(seq_peers):
            send(f_own.at[t], f_all.at[t, s], f_ss.at[t, i], f_rs.at[t, s], {"seq": p})
        if t == 0:
            for i, p in enumerate(head_peers):
                wait_arrival(l_all.at[p], l_ss.at[i], l_rs.at[p], {"head": p})
    for i, p in enumerate(seq_peers):
        wait_arrival(f_all.at[1, p], f_ss.at[1, i], f_rs.at[1, p], {"seq": p})
    for i, p in enumerate(head_peers):
        send(f_all.at[1], g_all.at[1, c], g_ss.at[1, i], g_rs.at[1, c], {"head": p})
    g_all[1, c] = f_all[1]
    for i, p in enumerate(head_peers):
        wait_arrival(g_all.at[1, p], g_ss.at[1, i], g_rs.at[1, p], {"head": p})
    for i in range(8):
        for j in range(4):
            cols = slice(512 * i + 128 * j, 512 * i + 128 * j + 128)
            one_col = g_all[1, :, i, j, :]
            out_second[:, cols] = one_col
    stores.append(pltpu.make_async_copy(out_second, second_out, out_sem.at[2]))
    stores[2].start()
    for copy in sent:
        copy.wait_send()
    for copy in stores:
        copy.wait()


def on_device(
    enc_out, enc_gain, key_weight, value_weight, query_weight, out_weight,
    dec_gain, beam_state, parents, token_embed,
):
    anywhere = pl.BlockSpec(memory_space=pl.ANY)
    f32, bf16 = jnp.float32, jnp.bfloat16
    dma = pltpu.SemaphoreType.DMA
    rows = jax.ShapeDtypeStruct((BEAMS, 4096), f32)

    def pair(*shape):
        return [dma(shape), dma(shape)]

    before, once, twice = pl.pallas_call(
        kernel,
        out_shape=(rows, rows, rows),
        in_specs=[anywhere] * 8 + [pl.BlockSpec(memory_space=pltpu.SMEM), anywhere],
        out_specs=(anywhere, anywhere, anywhere),
        scratch_shapes=[
            pltpu.VMEM((1, 4096), f32),
            pltpu.VMEM((512, 256), bf16),
            pltpu.VMEM((256, 512), bf16),
            pltpu.VMEM((1, 4096), f32),
            pltpu.VMEM((BEAMS, 4096), f32),
            pltpu.VMEM((STEPS, BEAMS, 4096), bf16),
            pltpu.VMEM((BEAMS, 4096), f32),
            pltpu.VMEM((BEAMS, 4096), f32),
            pltpu.VMEM((BEAMS, 4096), f32),
            pltpu.VMEM((HEAD, 512, 256), bf16),
            pltpu.VMEM((512, 4096), bf16),
            pltpu.VMEM((4, 4096, 256), bf16),
            pltpu.VMEM((4, 512, 256), bf16),
            pltpu.VMEM((BEAMS, 4096), f32),
            pltpu.VMEM((BEAMS, 512), f32),
            pltpu.VMEM((BEAMS, 4096), f32),
            pltpu.VMEM((BEAMS, 512), f32),
            pltpu.VMEM((BEAMS, 4096), f32),
            pltpu.VMEM((STEPS, BEAMS, 256), f32),
            pltpu.VMEM((STEPS, 8, BEAMS, 256), f32),
            pltpu.VMEM((STEPS, 2, BEAMS, 256), f32),
            pltpu.VMEM((STEPS, 2, 2, BEAMS, 256), f32),
            pltpu.VMEM((1, 128), f32),
            pltpu.VMEM((8, 1, 128), f32),
            pltpu.VMEM((1, 128), f32),
            pltpu.VMEM((2, 1, 128), f32),
            pltpu.VMEM((STEPS, 2, BEAMS, 256), bf16),
            pltpu.VMEM((STEPS, 8, BEAMS, 256), bf16),
            pltpu.VMEM((STEPS, 2, 1, 128), f32),
            pltpu.VMEM((STEPS, 8, 1, 128), f32),
            pltpu.VMEM((STEPS, 8, 128), f32),
            pltpu.VMEM((STEPS, 2, 8, 128), f32),
            pltpu.VMEM((STEPS, BEAMS, 256), f32),
            pltpu.VMEM((STEPS, 2, BEAMS, 256), f32),
            pltpu.VMEM((STEPS, BEAMS, 4, 128), f32),
            pltpu.VMEM((STEPS, HEAD, 4, 128), f32),
            pltpu.VMEM((STEPS, 4, 128), f32),
            pltpu.VMEM((STEPS, SEQ, 4, 128), f32),
            pltpu.VMEM((BEAMS, 4, 128), f32),
            pltpu.VMEM((STEPS, BEAMS, 8, 4, 128), f32),
            dma((3,)), dma((6,)), dma((3,)),
            *pair(8, 2), *pair(8, 2, 2), *pair(8, 2), *pair(8, 4), *pair(3, 2), *pair(4, 2, 2), *pair(4, 2),
            *pair(STEPS, 8), *pair(STEPS), *pair(8), *pair(1), *pair(STEPS, 8), *pair(STEPS, 8),
            *pair(STEPS), *pair(STEPS), *pair(STEPS, HEAD), *pair(STEPS, SEQ), *pair(HEAD), *pair(STEPS, HEAD),
        ],
        compiler_params=pltpu.CompilerParams(collective_id=1, has_side_effects=True),
        name="beam_decode",
    )(
        enc_out, enc_gain.reshape(1, 4096), key_weight, value_weight, query_weight, out_weight,
        dec_gain.reshape(1, 4096), beam_state, parents, token_embed,
    )
    return before + twice, once + twice


def solution(mesh):
    placed = (
        P(("src", "seq"), "head"),
        P(),
        P("seq", "head"),
        P("seq", "head"),
        P("seq", "head"),
        P("head", "seq"),
        P(),
        P("src", None),
        P("src", None),
        P("src", None, None),
    )
    return jax.shard_map(
        on_device,
        mesh=mesh,
        in_specs=placed,
        out_specs=(P("src", None), P("src", None)),
        check_vma=False,
    )
```

```python
import functools

import jax
import jax.numpy as jnp
from jax import lax
from jax.experimental import pallas as pl
from jax.experimental.pallas import tpu as pltpu
from jax.sharding import PartitionSpec as P

MESH = pl.DeviceIdType.MESH
HEAD_DIM = 64
BEAMS = 16
STEPS = 2
SEQ = 8
HEAD = 16


def place():
    y = lax.axis_index("src")
    s = lax.axis_index("seq")
    c = lax.axis_index("head")
    zh, k = lax.div(s, 2), lax.rem(s, 2)
    zl, x = lax.div(c, 4), lax.rem(c, 4)
    b, r = lax.rem(zl, 2), lax.div(zl, 2)
    return y, s, c, k, zl, x, b, r, zh * 2 + r


def node_id(m, k, b, x):
    return {"seq": lax.div(m, 2) * 2 + k, "head": (lax.rem(m, 2) * 2 + b) * 4 + x}


def partner_id(s, k):
    return {"seq": s + 1 - 2 * k}


def start_send(sent, src, dst, ss, rs, where):
    copy = pltpu.make_async_remote_copy(
        src_ref=src, dst_ref=dst, send_sem=ss, recv_sem=rs, device_id=where, device_id_type=MESH,
    )
    copy.start()
    sent.append(copy)


def wait_arrival(dst, ss, rs, where):
    pltpu.make_async_remote_copy(
        src_ref=dst, dst_ref=dst, send_sem=ss, recv_sem=rs, device_id=where, device_id_type=MESH,
    ).wait_recv()


OFFSETS = (0, -1, 1, -2, 2, -3, 3, 4)
BY_OFFSET = {off: q for q, off in enumerate(OFFSETS)}


def kernel(
    enc, enc_gain_in, wk, wv, wq_in, wo_in, gain_in, first_in, parents, tokens_in,
    pre_out, first_out, second_out,
    enc_gain, wq, wo, gain, first, tokens, out_pre, out_first, out_second,
    ebuf, nbuf, wbuf, kv,
    pre, part, picked, local_rows, full,
    q_own, q_all, w_own, w_all, u_own, u_all, z_own, z_all, zz_own, zz_all, c_own, c_all, t_own, t_all, m_own, m_all, v_own, v_all,
    p_own, p_all, f_own, f_all, l_all, g_all,
    own_sem, in_sem, out_sem, wz_ss, wz_rs, wy_ss, wy_rs, wh_ss, wh_rs, wc_ss, wc_rs, ez_ss, ez_rs, ex_ss, ex_rs, eh_ss, eh_rs,
    q_ss, q_rs, u_ss, u_rs, z_ss, z_rs, zz_ss, zz_rs, c_ss, c_rs, t_ss, t_rs, m_ss, m_rs, v_ss, v_rs,
    p_ss, p_rs, f_ss, f_rs, l_ss, l_rs, g_ss, g_rs, e_ss, e_rs,
):
    y, s, c, k, zl, x, b, r, n = place()
    up, down = {"src": lax.rem(y + 1, 4)}, {"src": lax.rem(y + 3, 4)}
    east = {"head": zl * 4 + lax.rem(x + 1, 4)}
    west = {"head": zl * 4 + lax.rem(x + 3, 4)}
    partner = partner_id(s, k)
    right = node_id(lax.rem(n + 1, 8), k, b, x)
    left = node_id(lax.rem(n + 7, 8), k, b, x)
    sibling = zl + 1 - 2 * b
    opposite = lax.rem(zl + 2, 4)
    quarters = [y, lax.rem(y + 3, 4), lax.rem(y + 1, 4), lax.rem(y + 2, 4)]

    def rows_of(m, quarter, core):
        return pl.ds(pl.multiple_of((lax.div(m, 2) * 2 + core) * 512 + quarter * 128, 128), 128)

    def nodes(q):
        return lax.rem(n + 8 + OFFSETS[q], 8)

    def both(q, j, core):
        m = nodes(q)
        return wbuf.at[pl.ds(2 * lax.rem(m, 2), 2), rows_of(m, quarters[j], core), :]

    def one(q, j, mat):
        m = nodes(q)
        return wbuf.at[2 * lax.rem(m, 2) + mat, rows_of(m, quarters[j], k), :]

    def shard(mat):
        at = pl.ds(pl.multiple_of(s * 512, 512), 512)
        return wbuf.at[2 * r + mat, at, :]

    def shard_both(core):
        at = pl.ds(pl.multiple_of((lax.div(n, 2) * 2 + core) * 512, 512), 512)
        return wbuf.at[pl.ds(2 * r, 2), at, :]

    def local(src, dst, i):
        copy = pltpu.make_async_copy(src, dst, own_sem.at[i])
        copy.start()
        return copy

    near = pl.ds(pl.multiple_of(r * 512, 512), 512)
    far = pl.ds(pl.multiple_of(512 - r * 512, 512), 512)
    seq_peers = [lax.rem(s + i, SEQ) for i in range(1, SEQ)]
    head_peers = [lax.rem(c + i, HEAD) for i in range(1, HEAD)]
    ring_peers = [lax.rem(n + i, 8) for i in range(1, 8)]
    other = 1 - k
    feats = pl.ds(pl.multiple_of(s * 512, 512), 512)

    def ring(m):
        return node_id(m, k, b, x)

    barrier = pltpu.get_barrier_semaphore()
    greet = [up, down, east, west, partner, right, left]
    greet += [{"head": sibling * 4 + x}, {"head": opposite * 4 + x}]
    for where in greet:
        pl.semaphore_signal(barrier, inc=1, device_id=where, device_id_type=MESH)
    locals_ = [
        local(wk, shard(0), 0),
        local(wv, shard(1), 1),
        local(enc.at[near, :], ebuf.at[c], 2),
    ]
    loads = [
        pltpu.make_async_copy(src, dst, in_sem.at[i])
        for i, (src, dst) in enumerate(
            (
                (first_in, first), (tokens_in, tokens), (gain_in, gain), (wq_in, wq),
                (enc_gain_in, enc_gain), (wo_in, wo),
            )
        )
    ]
    for copy in loads:
        copy.start()
    for copy in locals_:
        copy.wait()
    pl.semaphore_wait(barrier, len(greet))

    sent = []
    send = functools.partial(start_send, sent)

    def z_on(q, mat):
        off = OFFSETS[q]
        if -3 < off <= 0 or (off == -3 and mat == 0):
            t = 7 if off == -3 else BY_OFFSET[off - 1]
            send(one(q, 0, mat), one(q, 0, mat), wz_ss.at[t, mat], wz_rs.at[t, mat], right)
        if 0 <= off < 3 or (off == 3 and mat == 1):
            t = 7 if off == 3 else BY_OFFSET[off + 1]
            send(one(q, 0, mat), one(q, 0, mat), wz_ss.at[t, mat], wz_rs.at[t, mat], left)

    def z_step(q, mat):
        wait_arrival(one(q, 0, mat), wz_ss.at[q, mat], wz_rs.at[q, mat], right)
        z_on(q, mat)
        send(one(q, 0, mat), one(q, 0, mat), wy_ss.at[q, mat, 0], wy_rs.at[q, mat, 0], up)
        send(one(q, 0, mat), one(q, 0, mat), wy_ss.at[q, mat, 1], wy_rs.at[q, mat, 1], down)
        if mat == 1:
            cross(q, 0)

    def cross(q, j):
        send(both(q, j, k), both(q, j, k), wc_ss.at[q, j], wc_rs.at[q, j], partner)

    def y_relay(q):
        wait_arrival(one(q, 1, 0), wy_ss.at[q, 0, 0], wy_rs.at[q, 0, 0], up)
        send(one(q, 1, 0), one(q, 1, 0), wh_ss.at[q, 0], wh_rs.at[q, 0], up)
        wait_arrival(one(q, 2, 1), wy_ss.at[q, 1, 1], wy_rs.at[q, 1, 1], down)
        send(one(q, 2, 1), one(q, 2, 1), wh_ss.at[q, 1], wh_rs.at[q, 1], down)

    def y_cross(q):
        wait_arrival(one(q, 1, 1), wy_ss.at[q, 1, 0], wy_rs.at[q, 1, 0], up)
        cross(q, 1)
        wait_arrival(one(q, 2, 0), wy_ss.at[q, 0, 1], wy_rs.at[q, 0, 1], down)
        cross(q, 2)

    def y_last(q):
        wait_arrival(one(q, 3, 0), wh_ss.at[q, 0], wh_rs.at[q, 0], up)
        wait_arrival(one(q, 3, 1), wh_ss.at[q, 1], wh_rs.at[q, 1], down)
        cross(q, 3)

    piece_z = [zl, sibling, opposite, lax.rem(sibling + 2, 4)]
    xs = [x, lax.rem(x + 3, 4), lax.rem(x + 1, 4), lax.rem(x + 2, 4)]

    def half(p, xs_, i):
        return ebuf.at[piece_z[p] * 4 + xs_, pl.ds(256 * i, 256), :]

    def own_half(at, i):
        return enc.at[pl.ds(pl.multiple_of(at + 256 * i, 256), 256), :]

    def e_near(i):
        send(half(0, x, i), half(0, x, i), ez_ss.at[0, i], ez_rs.at[0, i], {"head": sibling * 4 + x})

    def e_far(i):
        send(own_half(512 - r * 512, i), half(0, x, i), ez_ss.at[1, i], ez_rs.at[1, i], {"head": opposite * 4 + x})

    def e_step(p, i):
        wait_arrival(half(p, x, i), ez_ss.at[p - 1, i], ez_rs.at[p - 1, i], east)
        if p == 2:
            send(half(2, x, i), half(2, x, i), ez_ss.at[2, i], ez_rs.at[2, i], {"head": sibling * 4 + x})
        x_out(p, i)

    def x_out(p, i):
        for d, where in ((0, east), (1, west)):
            send(half(p, x, i), half(p, x, i), ex_ss.at[p, i, d], ex_rs.at[p, i, d], where)

    def x_relay(p):
        wait_arrival(half(p, xs[1], 0), ex_ss.at[p, 0, 0], ex_rs.at[p, 0, 0], east)
        send(half(p, xs[1], 0), half(p, xs[1], 0), eh_ss.at[p, 0], eh_rs.at[p, 0], east)
        wait_arrival(half(p, xs[2], 1), ex_ss.at[p, 1, 1], ex_rs.at[p, 1, 1], west)
        send(half(p, xs[2], 1), half(p, xs[2], 1), eh_ss.at[p, 1], eh_rs.at[p, 1], west)

    def x_last(p):
        wait_arrival(half(p, xs[1], 1), ex_ss.at[p, 1, 0], ex_rs.at[p, 1, 0], east)
        wait_arrival(half(p, xs[2], 0), ex_ss.at[p, 0, 1], ex_rs.at[p, 0, 1], west)
        wait_arrival(half(p, xs[3], 0), eh_ss.at[p, 0], eh_rs.at[p, 0], east)
        wait_arrival(half(p, xs[3], 1), eh_ss.at[p, 1], eh_rs.at[p, 1], west)

    col_head = lax.broadcasted_iota(jnp.int32, (BEAMS, 256), 1) // HEAD_DIM
    lane = lax.broadcasted_iota(jnp.int32, (8, 128), 1)
    is_top = lax.rem(lane, 8) < 4

    def spread_rows(share):
        halves = []
        for half in range(2):
            scale = jnp.zeros((8, 256), jnp.float32)
            for h in range(4):
                at = 8 * half + h
                scale = jnp.where(
                    col_head[:8] == h, jnp.broadcast_to(share[:, at:at + 1], (8, 256)), scale
                )
            halves.append(scale)
        return jnp.concatenate(halves, axis=0)

    row_of = lax.broadcasted_iota(jnp.int32, (8, 128), 0)

    def swap_rows(tile, step):
        return jnp.where(
            lax.rem(lax.div(row_of, step), 2) == 0, pltpu.roll(tile, 8 - step, 0), pltpu.roll(tile, step, 0)
        )

    def fold(tile):
        turned = swap_rows(swap_rows(pltpu.roll(tile, 4, 0), 2), 1)
        return jnp.sum(pltpu.roll(turned, 0, 1, stride=16, stride_axis=0), axis=0, keepdims=True)

    def unfold(row):
        return pltpu.roll(jnp.broadcast_to(row, (8, 128)), 16, 1, stride=16, stride_axis=0)

    def merge(stats, parts):
        peak = functools.reduce(jnp.maximum, stats)
        factors = [jnp.exp(one - peak) for one in stats]
        sums = functools.reduce(
            lambda a, b: a + b, [f * pltpu.roll(one, 124, 1) for f, one in zip(factors, stats)]
        )
        joined = functools.reduce(
            lambda a, b: a + b, [one * spread_rows(f) for f, one in zip(factors, parts)]
        )
        return peak, sums, joined

    def query_out(t):
        for i in (3, 2, 4, 1, 5, 0, 6):
            m = ring_peers[i]
            if t == 1:
                send(z_own, z_all.at[n], z_ss.at[i], z_rs.at[n], ring(m))
            mine, theirs = (w_own, w_all) if t == 1 else (q_own, q_all)
            send(mine, theirs.at[n], q_ss.at[t, i], q_rs.at[t, n], ring(m))

    def query_swap(t):
        for i, m in enumerate(ring_peers):
            if t == 1:
                wait_arrival(z_all.at[m], z_ss.at[i], z_rs.at[m], ring(m))
            wait_arrival((w_all if t == 1 else q_all).at[m], q_ss.at[t, i], q_rs.at[t, m], ring(m))
        if t == 1:
            squares = (z_all[0] + z_all[2]) + (z_all[4] + z_all[6])
            zz_own[...] = squares
            zz_all[k] = squares
            send(zz_own, zz_all.at[k], zz_ss.at[0], zz_rs.at[0], partner)
        for g in range(2):
            source = w_all if t == 1 else q_all
            each = [source[m].astype(jnp.float32) for m in range(g, 8, 2)]
            both_g = (each[0] + each[1]) + (each[2] + each[3])
            u_all[t, k, g] = both_g
            u_own[t, g] = both_g
        send(u_own.at[t], u_all.at[t, k], u_ss.at[t], u_rs.at[t], partner)

    def query_in(t):
        if t == 1:
            wait_arrival(zz_all.at[other], zz_ss.at[0], zz_rs.at[0], partner)
        wait_arrival(u_all.at[t, other], u_ss.at[t], u_rs.at[t], partner)

    def attend(t, g, scale):
        query = u_all[t, 0, g] + u_all[t, 1, g]
        if scale is not None:
            query = query * scale
        query = query.astype(jnp.bfloat16).astype(jnp.float32)
        spread = jnp.concatenate(
            [jnp.where(col_head == h, query, 0.0) for h in range(4)], axis=0
        ).astype(jnp.bfloat16)
        scores = lax.dot_general(
            spread, kv[2 * g], (((1,), (1,)), ((), ())), preferred_element_type=jnp.float32
        ) * 0.125
        top = jnp.max(scores, axis=-1, keepdims=True)
        expo = jnp.exp(scores - top)
        total = jnp.sum(expo, axis=-1, keepdims=True)
        mixed = jnp.dot(expo.astype(jnp.bfloat16), kv[2 * g + 1], preferred_element_type=jnp.float32)
        ctx = jnp.zeros((BEAMS, 256), jnp.float32)
        stats = jnp.zeros((8, 128), jnp.float32)
        for h in range(4):
            ctx += jnp.where(col_head == h, mixed[16 * h:16 * h + 16], 0.0)
            for half in range(2):
                at = 16 * h + 8 * half
                stats = jnp.where(lane == 8 * half + h, top[at:at + 8], stats)
                stats = jnp.where(lane == 8 * half + 4 + h, total[at:at + 8], stats)
        return ctx.astype(jnp.bfloat16), stats

    z_on(0, 0)
    z_on(0, 1)
    e_near(0)
    e_far(0)
    e_near(1)
    e_far(1)
    x_out(0, 0)
    x_out(0, 1)
    send(shard_both(k), shard_both(k), wc_ss.at[0, 0], wc_rs.at[0, 0], partner)

    for copy in loads:
        copy.wait()
    for i in range(BEAMS):
        picked[pl.ds(i, 1), :] = first[pl.ds(parents[0, i], 1), :]
    start = picked[...] + tokens[0].astype(jnp.float32)
    pre[...] = start
    mean = jnp.sum(start * start, axis=-1, keepdims=True) * (1.0 / 4096.0)
    picked[...] = start * lax.rsqrt(mean + 1e-06) * gain[...]
    q_own[...] = jnp.dot(picked[:, feats].astype(jnp.bfloat16), wq[...], preferred_element_type=jnp.float32)
    q_all[n] = q_own[...]

    z_step(1, 0)
    z_step(2, 0)
    z_step(1, 1)
    z_step(2, 1)
    x_relay(0)
    e_step(1, 0)
    e_step(1, 1)
    z_step(3, 0)
    z_step(4, 0)
    z_step(3, 1)
    z_step(4, 1)
    e_step(2, 0)
    e_step(2, 1)
    y_relay(1)
    y_relay(2)
    x_relay(1)
    z_step(5, 0)
    z_step(6, 0)
    z_step(5, 1)
    z_step(6, 1)
    x_last(0)
    y_relay(3)
    y_relay(4)
    y_cross(1)
    y_cross(2)
    x_relay(2)
    x_last(1)
    e_step(3, 0)
    e_step(3, 1)
    z_step(7, 0)
    z_step(7, 1)
    query_out(0)
    y_last(1)
    y_last(2)
    y_relay(5)
    y_relay(6)
    y_cross(3)
    y_cross(4)
    x_relay(3)
    y_last(3)
    y_last(4)
    x_last(2)
    y_relay(7)
    y_cross(5)
    y_cross(6)
    y_last(5)
    y_last(6)
    x_last(3)

    @pl.loop(0, 8)
    def _(i):
        at = pl.ds(pl.multiple_of(i * 64, 64), 64)
        acc = jnp.zeros((64, 128), jnp.float32)
        for f in range(HEAD):
            block = ebuf[f, at, :].astype(jnp.float32)
            block = block * block
            acc += block[:, :128] + block[:, 128:]
        scale = lax.rsqrt(jnp.sum(acc, axis=-1, keepdims=True) * (1.0 / 4096.0) + 1e-06)
        for f in range(HEAD):
            cols = slice(256 * f, 256 * f + 256)
            block = ebuf[f, at, :].astype(jnp.float32) * scale * enc_gain[:, cols]
            nbuf[at, cols] = block.astype(jnp.bfloat16)

    y_cross(7)
    y_last(7)
    query_swap(0)
    wait_arrival(shard_both(other), wc_ss.at[0, 0], wc_rs.at[0, 0], partner)
    for q in range(1, 8):
        for j in range(4):
            wait_arrival(both(q, j, other), wc_ss.at[q, j], wc_rs.at[q, j], partner)

    @pl.loop(0, 4)
    def _(i):
        kv[i] = jnp.dot(nbuf[...], wbuf[i], preferred_element_type=jnp.float32).astype(jnp.bfloat16)

    for t in range(STEPS):
        scale = None
        if t == 1:
            for j in range(4):
                part[:, 128 * j:128 * j + 128] = l_all[:, j, :]
            part[...] = part[...] + pre[:, feats]
            for i in range(BEAMS):
                local_rows[pl.ds(i, 1), :] = part[pl.ds(parents[1, i], 1), :]
            rows = local_rows[...] + tokens[1, :, feats].astype(jnp.float32)
            squares = jnp.sum(rows * rows, axis=-1, keepdims=True)
            z_own[...] = fold(
                jnp.where(lane == 0, squares[:8], jnp.where(lane == 1, squares[8:], 0.0))
            )
            z_all[n] = z_own[...]
            scaled = rows * gain[:, feats]
            high = scaled.astype(jnp.bfloat16)
            low = (scaled - high.astype(jnp.float32)).astype(jnp.bfloat16)
            partial = jnp.dot(high, wq[...], preferred_element_type=jnp.float32) + jnp.dot(
                low, wq[...], preferred_element_type=jnp.float32
            )
            w_own[...] = partial.astype(jnp.bfloat16)
            w_all[n] = w_own[...]
            query_out(1)
            query_swap(1)
            for i, p in enumerate(seq_peers):
                wait_arrival(f_all.at[0, p], f_ss.at[0, i], f_rs.at[0, p], {"seq": p})
            for i, p in enumerate(head_peers):
                send(f_all.at[0], g_all.at[0, c], g_ss.at[0, i], g_rs.at[0, c], {"head": p})
            g_all[0, c] = f_all[0]
        query_in(t)
        if t == 1:
            table = lax.rsqrt(unfold(zz_all[0] + zz_all[1]) * (1.0 / 4096.0) + 1e-06)
            scale = jnp.concatenate([table[:, :1], table[:, 1:2]], axis=0)
        for slot, g, order in ((1, r, (3, 1, 5)), (0, 1 - r, (2, 4, 0, 6))):
            ctx, stats = attend(t, g, scale)
            c_own[t, slot] = ctx
            t_own[t, slot] = fold(stats)
            for i in order:
                m = ring_peers[i]
                send(t_own.at[t, slot], t_all.at[t, n], t_ss.at[t, i], t_rs.at[t, n], ring(m))
                send(c_own.at[t, slot], c_all.at[t, n], c_ss.at[t, i], c_rs.at[t, n], ring(m))
        c_all[t, n] = c_own[t, 1]
        t_all[t, n] = t_own[t, 1]
        if t == 1:
            for i, p in enumerate(head_peers):
                wait_arrival(g_all.at[0, p], g_ss.at[0, i], g_rs.at[0, p], {"head": p})
            for i in range(8):
                for j in range(4):
                    cols = slice(512 * i + 128 * j, 512 * i + 128 * j + 128)
                    one_col = g_all[0, :, i, j, :]
                    out_first[:, cols] = one_col
                    full[:, cols] = pre[:, cols] + one_col
            for i in range(BEAMS):
                picked[pl.ds(i, 1), :] = full[pl.ds(parents[1, i], 1), :]
            out_pre[...] = picked[...] + tokens[1].astype(jnp.float32)
            stores = [
                pltpu.make_async_copy(out_pre, pre_out, out_sem.at[0]),
                pltpu.make_async_copy(out_first, first_out, out_sem.at[1]),
            ]
            for copy in stores:
                copy.start()
        for i, m in enumerate(ring_peers):
            wait_arrival(t_all.at[t, m], t_ss.at[t, i], t_rs.at[t, m], ring(m))
            wait_arrival(c_all.at[t, m], c_ss.at[t, i], c_rs.at[t, m], ring(m))
        peak, sums, joined = merge(
            [unfold(t_all[t, i]) for i in range(8)], [c_all[t, i].astype(jnp.float32) for i in range(8)]
        )
        stats = jnp.where(is_top, peak, pltpu.roll(sums, 4, 1))
        v_own[t] = joined
        m_own[t] = stats
        v_all[t, k] = joined
        m_all[t, k] = stats
        send(m_own.at[t], m_all.at[t, k], m_ss.at[t], m_rs.at[t], partner)
        send(v_own.at[t], v_all.at[t, k], v_ss.at[t], v_rs.at[t], partner)
        wait_arrival(m_all.at[t, other], m_ss.at[t], m_rs.at[t], partner)
        wait_arrival(v_all.at[t, other], v_ss.at[t], v_rs.at[t], partner)
        peak, sums, joined = merge([m_all[t, 0], m_all[t, 1]], [v_all[t, 0], v_all[t, 1]])
        context = (joined / spread_rows(sums)).astype(jnp.bfloat16)
        partial = jnp.dot(context, wo[...], preferred_element_type=jnp.float32)
        for j in range(4):
            p_own[t, :, j, :] = partial[:, 128 * j:128 * j + 128]
        p_all[t, c] = p_own[t, c]
        for i, p in enumerate(head_peers):
            send(p_own.at[t, p], p_all.at[t, c], p_ss.at[t, i], p_rs.at[t, c], {"head": p})
        for i, p in enumerate(head_peers):
            wait_arrival(p_all.at[t, p], p_ss.at[t, i], p_rs.at[t, p], {"head": p})
        row = p_all[t, 0]
        for i in range(1, HEAD):
            row += p_all[t, i]
        f_own[t] = row
        f_all[t, s] = row
        if t == 0:
            for i, p in enumerate(head_peers):
                send(f_own.at[t], l_all.at[c], l_ss.at[i], l_rs.at[c], {"head": p})
            l_all[c] = row
        for i, p in enumerate(seq_peers):
            send(f_own.at[t], f_all.at[t, s], f_ss.at[t, i], f_rs.at[t, s], {"seq": p})
        if t == 0:
            for i, p in enumerate(head_peers):
                wait_arrival(l_all.at[p], l_ss.at[i], l_rs.at[p], {"head": p})
    z_hi = lax.div(s, 2)
    slices = [lax.rem(z_hi + i, 4) for i in (0, 1, 3, 2)]
    for i, z_from in enumerate(slices):
        for core in (0, 1):
            if i == 0:
                continue
            p = 2 * z_from + core
            wait_arrival(f_all.at[1, p], f_ss.at[1, 0], f_rs.at[1, p], partner)
        if i == 0:
            wait_arrival(f_all.at[1, s + 1 - 2 * k], f_ss.at[1, 0], f_rs.at[1, s + 1 - 2 * k], partner)
        two = pl.ds(2 * z_from, 2)
        for h, p in enumerate(head_peers):
            send(f_all.at[1, two], g_all.at[1, c, two], e_ss.at[i, h], e_rs.at[i, c], {"head": p})
    g_all[1, c] = f_all[1]
    for i, z_from in enumerate(slices):
        two = pl.ds(2 * z_from, 2)
        for h, p in enumerate(head_peers):
            wait_arrival(g_all.at[1, p, two], e_ss.at[i, h], e_rs.at[i, p], {"head": p})
    for i in range(8):
        for j in range(4):
            cols = slice(512 * i + 128 * j, 512 * i + 128 * j + 128)
            one_col = g_all[1, :, i, j, :]
            out_second[:, cols] = one_col
    stores.append(pltpu.make_async_copy(out_second, second_out, out_sem.at[2]))
    stores[2].start()
    for copy in sent:
        copy.wait_send()
    for copy in stores:
        copy.wait()


def on_device(
    enc_out, enc_gain, key_weight, value_weight, query_weight, out_weight,
    dec_gain, beam_state, parents, token_embed,
):
    anywhere = pl.BlockSpec(memory_space=pl.ANY)
    f32, bf16 = jnp.float32, jnp.bfloat16
    dma = pltpu.SemaphoreType.DMA
    rows = jax.ShapeDtypeStruct((BEAMS, 4096), f32)

    def pair(*shape):
        return [dma(shape), dma(shape)]

    before, once, twice = pl.pallas_call(
        kernel,
        out_shape=(rows, rows, rows),
        in_specs=[anywhere] * 8 + [pl.BlockSpec(memory_space=pltpu.SMEM), anywhere],
        out_specs=(anywhere, anywhere, anywhere),
        scratch_shapes=[
            pltpu.VMEM((1, 4096), f32),
            pltpu.VMEM((512, 256), bf16),
            pltpu.VMEM((256, 512), bf16),
            pltpu.VMEM((1, 4096), f32),
            pltpu.VMEM((BEAMS, 4096), f32),
            pltpu.VMEM((STEPS, BEAMS, 4096), bf16),
            pltpu.VMEM((BEAMS, 4096), f32),
            pltpu.VMEM((BEAMS, 4096), f32),
            pltpu.VMEM((BEAMS, 4096), f32),
            pltpu.VMEM((HEAD, 512, 256), bf16),
            pltpu.VMEM((512, 4096), bf16),
            pltpu.VMEM((4, 4096, 256), bf16),
            pltpu.VMEM((4, 512, 256), bf16),
            pltpu.VMEM((BEAMS, 4096), f32),
            pltpu.VMEM((BEAMS, 512), f32),
            pltpu.VMEM((BEAMS, 4096), f32),
            pltpu.VMEM((BEAMS, 512), f32),
            pltpu.VMEM((BEAMS, 4096), f32),
            pltpu.VMEM((BEAMS, 256), f32),
            pltpu.VMEM((8, BEAMS, 256), f32),
            pltpu.VMEM((BEAMS, 256), bf16),
            pltpu.VMEM((8, BEAMS, 256), bf16),
            pltpu.VMEM((STEPS, 2, BEAMS, 256), f32),
            pltpu.VMEM((STEPS, 2, 2, BEAMS, 256), f32),
            pltpu.VMEM((1, 128), f32),
            pltpu.VMEM((8, 1, 128), f32),
            pltpu.VMEM((1, 128), f32),
            pltpu.VMEM((2, 1, 128), f32),
            pltpu.VMEM((STEPS, 2, BEAMS, 256), bf16),
            pltpu.VMEM((STEPS, 8, BEAMS, 256), bf16),
            pltpu.VMEM((STEPS, 2, 1, 128), f32),
            pltpu.VMEM((STEPS, 8, 1, 128), f32),
            pltpu.VMEM((STEPS, 8, 128), f32),
            pltpu.VMEM((STEPS, 2, 8, 128), f32),
            pltpu.VMEM((STEPS, BEAMS, 256), f32),
            pltpu.VMEM((STEPS, 2, BEAMS, 256), f32),
            pltpu.VMEM((STEPS, BEAMS, 4, 128), f32),
            pltpu.VMEM((STEPS, HEAD, 4, 128), f32),
            pltpu.VMEM((STEPS, 4, 128), f32),
            pltpu.VMEM((STEPS, SEQ, 4, 128), f32),
            pltpu.VMEM((BEAMS, 4, 128), f32),
            pltpu.VMEM((STEPS, BEAMS, 8, 4, 128), f32),
            dma((3,)), dma((6,)), dma((3,)),
            *pair(8, 2), *pair(8, 2, 2), *pair(8, 2), *pair(8, 4), *pair(3, 2), *pair(4, 2, 2), *pair(4, 2),
            *pair(STEPS, 8), *pair(STEPS), *pair(8), *pair(1), *pair(STEPS, 8), *pair(STEPS, 8),
            *pair(STEPS), *pair(STEPS), *pair(STEPS, HEAD), *pair(STEPS, SEQ), *pair(HEAD), *pair(STEPS, HEAD), *pair(4, HEAD),
        ],
        compiler_params=pltpu.CompilerParams(collective_id=1, has_side_effects=True),
        name="beam_decode",
    )(
        enc_out, enc_gain.reshape(1, 4096), key_weight, value_weight, query_weight, out_weight,
        dec_gain.reshape(1, 4096), beam_state, parents, token_embed,
    )
    return before + twice, once + twice


def solution(mesh):
    placed = (
        P(("src", "seq"), "head"),
        P(),
        P("seq", "head"),
        P("seq", "head"),
        P("seq", "head"),
        P("head", "seq"),
        P(),
        P("src", None),
        P("src", None),
        P("src", None, None),
    )
    return jax.shard_map(
        on_device,
        mesh=mesh,
        in_specs=placed,
        out_specs=(P("src", None), P("src", None)),
        check_vma=False,
    )
```

```python
import functools

import jax
import jax.numpy as jnp
from jax import lax
from jax.experimental import pallas as pl
from jax.experimental.pallas import tpu as pltpu
from jax.sharding import PartitionSpec as P

MESH = pl.DeviceIdType.MESH
HEAD_DIM = 64
BEAMS = 16
STEPS = 2
SEQ = 8
HEAD = 16


def place():
    y = lax.axis_index("src")
    s = lax.axis_index("seq")
    c = lax.axis_index("head")
    zh, k = lax.div(s, 2), lax.rem(s, 2)
    zl, x = lax.div(c, 4), lax.rem(c, 4)
    b, r = lax.rem(zl, 2), lax.div(zl, 2)
    return y, s, c, k, zl, x, b, r, zh * 2 + r


def node_id(m, k, b, x):
    return {"seq": lax.div(m, 2) * 2 + k, "head": (lax.rem(m, 2) * 2 + b) * 4 + x}


def partner_id(s, k):
    return {"seq": s + 1 - 2 * k}


def start_send(sent, src, dst, ss, rs, where):
    copy = pltpu.make_async_remote_copy(
        src_ref=src, dst_ref=dst, send_sem=ss, recv_sem=rs, device_id=where, device_id_type=MESH,
    )
    copy.start()
    sent.append(copy)


def wait_arrival(dst, ss, rs, where):
    pltpu.make_async_remote_copy(
        src_ref=dst, dst_ref=dst, send_sem=ss, recv_sem=rs, device_id=where, device_id_type=MESH,
    ).wait_recv()


OFFSETS = (0, -1, 1, -2, 2, -3, 3, 4)
BY_OFFSET = {off: q for q, off in enumerate(OFFSETS)}


def kernel(
    enc, enc_gain_in, wk, wv, wq_in, wo_in, gain_in, first_in, parents, tokens_in,
    pre_out, first_out, second_out,
    enc_gain, wq, wo, gain, first, tokens, out_pre, out_first, out_second,
    ebuf, nbuf, wbuf, kv,
    pre, part, picked, local_rows, full,
    q_own, q_all, w_own, w_all, u_own, u_all, z_own, z_all, zz_own, zz_all, c_own, c_all, t_own, t_all, m_own, m_all, v_own, v_all,
    p_own, p_all, f_own, f_all, l_all, g_all,
    own_sem, in_sem, out_sem, wz_ss, wz_rs, wy_ss, wy_rs, wh_ss, wh_rs, wc_ss, wc_rs, ez_ss, ez_rs, ex_ss, ex_rs, eh_ss, eh_rs,
    q_ss, q_rs, u_ss, u_rs, z_ss, z_rs, zz_ss, zz_rs, c_ss, c_rs, t_ss, t_rs, m_ss, m_rs, v_ss, v_rs,
    p_ss, p_rs, f_ss, f_rs, l_ss, l_rs, g_ss, g_rs, e_ss, e_rs,
):
    y, s, c, k, zl, x, b, r, n = place()
    up, down = {"src": lax.rem(y + 1, 4)}, {"src": lax.rem(y + 3, 4)}
    east = {"head": zl * 4 + lax.rem(x + 1, 4)}
    west = {"head": zl * 4 + lax.rem(x + 3, 4)}
    partner = partner_id(s, k)
    right = node_id(lax.rem(n + 1, 8), k, b, x)
    left = node_id(lax.rem(n + 7, 8), k, b, x)
    sibling = zl + 1 - 2 * b
    opposite = lax.rem(zl + 2, 4)
    quarters = [y, lax.rem(y + 3, 4), lax.rem(y + 1, 4), lax.rem(y + 2, 4)]

    def rows_of(m, quarter, core):
        return pl.ds(pl.multiple_of((lax.div(m, 2) * 2 + core) * 512 + quarter * 128, 128), 128)

    def nodes(q):
        return lax.rem(n + 8 + OFFSETS[q], 8)

    def both(q, j, core):
        m = nodes(q)
        return wbuf.at[pl.ds(2 * lax.rem(m, 2), 2), rows_of(m, quarters[j], core), :]

    def one(q, j, mat):
        m = nodes(q)
        return wbuf.at[2 * lax.rem(m, 2) + mat, rows_of(m, quarters[j], k), :]

    def shard(mat):
        at = pl.ds(pl.multiple_of(s * 512, 512), 512)
        return wbuf.at[2 * r + mat, at, :]

    def shard_both(core):
        at = pl.ds(pl.multiple_of((lax.div(n, 2) * 2 + core) * 512, 512), 512)
        return wbuf.at[pl.ds(2 * r, 2), at, :]

    def local(src, dst, i):
        copy = pltpu.make_async_copy(src, dst, own_sem.at[i])
        copy.start()
        return copy

    near = pl.ds(pl.multiple_of(r * 512, 512), 512)
    far = pl.ds(pl.multiple_of(512 - r * 512, 512), 512)
    seq_peers = [lax.rem(s + i, SEQ) for i in range(1, SEQ)]
    head_peers = [lax.rem(c + i, HEAD) for i in range(1, HEAD)]
    ring_peers = [lax.rem(n + i, 8) for i in range(1, 8)]
    other = 1 - k
    feats = pl.ds(pl.multiple_of(s * 512, 512), 512)

    def ring(m):
        return node_id(m, k, b, x)

    barrier = pltpu.get_barrier_semaphore()
    greet = [up, down, east, west, partner, right, left]
    greet += [{"head": sibling * 4 + x}, {"head": opposite * 4 + x}]
    for where in greet:
        pl.semaphore_signal(barrier, inc=1, device_id=where, device_id_type=MESH)
    locals_ = [
        local(wk, shard(0), 0),
        local(wv, shard(1), 1),
        local(enc.at[near, :], ebuf.at[c], 2),
    ]
    loads = [
        pltpu.make_async_copy(src, dst, in_sem.at[i])
        for i, (src, dst) in enumerate(
            (
                (first_in, first), (tokens_in, tokens), (gain_in, gain), (wq_in, wq),
                (enc_gain_in, enc_gain), (wo_in, wo),
            )
        )
    ]
    for copy in loads:
        copy.start()
    for copy in locals_:
        copy.wait()
    pl.semaphore_wait(barrier, len(greet))

    sent = []
    send = functools.partial(start_send, sent)

    def z_on(q, mat):
        off = OFFSETS[q]
        if -3 < off <= 0 or (off == -3 and mat == 0):
            t = 7 if off == -3 else BY_OFFSET[off - 1]
            send(one(q, 0, mat), one(q, 0, mat), wz_ss.at[t, mat], wz_rs.at[t, mat], right)
        if 0 <= off < 3 or (off == 3 and mat == 1):
            t = 7 if off == 3 else BY_OFFSET[off + 1]
            send(one(q, 0, mat), one(q, 0, mat), wz_ss.at[t, mat], wz_rs.at[t, mat], left)

    def z_step(q, mat):
        wait_arrival(one(q, 0, mat), wz_ss.at[q, mat], wz_rs.at[q, mat], right)
        z_on(q, mat)
        send(one(q, 0, mat), one(q, 0, mat), wy_ss.at[q, mat, 0], wy_rs.at[q, mat, 0], up)
        send(one(q, 0, mat), one(q, 0, mat), wy_ss.at[q, mat, 1], wy_rs.at[q, mat, 1], down)
        if mat == 1:
            cross(q, 0)

    def cross(q, j):
        send(both(q, j, k), both(q, j, k), wc_ss.at[q, j], wc_rs.at[q, j], partner)

    def y_relay(q):
        wait_arrival(one(q, 1, 0), wy_ss.at[q, 0, 0], wy_rs.at[q, 0, 0], up)
        send(one(q, 1, 0), one(q, 1, 0), wh_ss.at[q, 0], wh_rs.at[q, 0], up)
        wait_arrival(one(q, 2, 1), wy_ss.at[q, 1, 1], wy_rs.at[q, 1, 1], down)
        send(one(q, 2, 1), one(q, 2, 1), wh_ss.at[q, 1], wh_rs.at[q, 1], down)

    def y_cross(q):
        wait_arrival(one(q, 1, 1), wy_ss.at[q, 1, 0], wy_rs.at[q, 1, 0], up)
        cross(q, 1)
        wait_arrival(one(q, 2, 0), wy_ss.at[q, 0, 1], wy_rs.at[q, 0, 1], down)
        cross(q, 2)

    def y_last(q):
        wait_arrival(one(q, 3, 0), wh_ss.at[q, 0], wh_rs.at[q, 0], up)
        wait_arrival(one(q, 3, 1), wh_ss.at[q, 1], wh_rs.at[q, 1], down)
        cross(q, 3)

    piece_z = [zl, sibling, opposite, lax.rem(sibling + 2, 4)]
    xs = [x, lax.rem(x + 3, 4), lax.rem(x + 1, 4), lax.rem(x + 2, 4)]

    def half(p, xs_, i):
        return ebuf.at[piece_z[p] * 4 + xs_, pl.ds(256 * i, 256), :]

    def own_half(at, i):
        return enc.at[pl.ds(pl.multiple_of(at + 256 * i, 256), 256), :]

    def e_near(i):
        send(half(0, x, i), half(0, x, i), ez_ss.at[0, i], ez_rs.at[0, i], {"head": sibling * 4 + x})

    def e_far(i):
        send(own_half(512 - r * 512, i), half(0, x, i), ez_ss.at[1, i], ez_rs.at[1, i], {"head": opposite * 4 + x})

    def e_step(p, i):
        wait_arrival(half(p, x, i), ez_ss.at[p - 1, i], ez_rs.at[p - 1, i], east)
        if p == 2:
            send(half(2, x, i), half(2, x, i), ez_ss.at[2, i], ez_rs.at[2, i], {"head": sibling * 4 + x})
        x_out(p, i)

    def x_out(p, i):
        for d, where in ((0, east), (1, west)):
            send(half(p, x, i), half(p, x, i), ex_ss.at[p, i, d], ex_rs.at[p, i, d], where)

    def x_relay(p):
        wait_arrival(half(p, xs[1], 0), ex_ss.at[p, 0, 0], ex_rs.at[p, 0, 0], east)
        send(half(p, xs[1], 0), half(p, xs[1], 0), eh_ss.at[p, 0], eh_rs.at[p, 0], east)
        wait_arrival(half(p, xs[2], 1), ex_ss.at[p, 1, 1], ex_rs.at[p, 1, 1], west)
        send(half(p, xs[2], 1), half(p, xs[2], 1), eh_ss.at[p, 1], eh_rs.at[p, 1], west)

    def x_last(p):
        wait_arrival(half(p, xs[1], 1), ex_ss.at[p, 1, 0], ex_rs.at[p, 1, 0], east)
        wait_arrival(half(p, xs[2], 0), ex_ss.at[p, 0, 1], ex_rs.at[p, 0, 1], west)
        wait_arrival(half(p, xs[3], 0), eh_ss.at[p, 0], eh_rs.at[p, 0], east)
        wait_arrival(half(p, xs[3], 1), eh_ss.at[p, 1], eh_rs.at[p, 1], west)

    col_head = lax.broadcasted_iota(jnp.int32, (BEAMS, 256), 1) // HEAD_DIM
    lane = lax.broadcasted_iota(jnp.int32, (8, 128), 1)
    is_top = lax.rem(lane, 8) < 4

    def spread_rows(share):
        halves = []
        for half in range(2):
            scale = jnp.zeros((8, 256), jnp.float32)
            for h in range(4):
                at = 8 * half + h
                scale = jnp.where(
                    col_head[:8] == h, jnp.broadcast_to(share[:, at:at + 1], (8, 256)), scale
                )
            halves.append(scale)
        return jnp.concatenate(halves, axis=0)

    row_of = lax.broadcasted_iota(jnp.int32, (8, 128), 0)

    def swap_rows(tile, step):
        return jnp.where(
            lax.rem(lax.div(row_of, step), 2) == 0, pltpu.roll(tile, 8 - step, 0), pltpu.roll(tile, step, 0)
        )

    def fold(tile):
        turned = swap_rows(swap_rows(pltpu.roll(tile, 4, 0), 2), 1)
        return jnp.sum(pltpu.roll(turned, 0, 1, stride=16, stride_axis=0), axis=0, keepdims=True)

    def unfold(row):
        return pltpu.roll(jnp.broadcast_to(row, (8, 128)), 16, 1, stride=16, stride_axis=0)

    def merge(stats, parts):
        peak = functools.reduce(jnp.maximum, stats)
        factors = [jnp.exp(one - peak) for one in stats]
        sums = functools.reduce(
            lambda a, b: a + b, [f * pltpu.roll(one, 124, 1) for f, one in zip(factors, stats)]
        )
        joined = functools.reduce(
            lambda a, b: a + b, [one * spread_rows(f) for f, one in zip(factors, parts)]
        )
        return peak, sums, joined

    def query_out(t):
        for i in (3, 2, 4, 1, 5, 0, 6):
            m = ring_peers[i]
            if t == 1:
                send(z_own, z_all.at[n], z_ss.at[i], z_rs.at[n], ring(m))
            mine, theirs = (w_own, w_all) if t == 1 else (q_own, q_all)
            send(mine, theirs.at[n], q_ss.at[t, i], q_rs.at[t, n], ring(m))

    def query_swap(t):
        for i, m in enumerate(ring_peers):
            if t == 1:
                wait_arrival(z_all.at[m], z_ss.at[i], z_rs.at[m], ring(m))
            wait_arrival((w_all if t == 1 else q_all).at[m], q_ss.at[t, i], q_rs.at[t, m], ring(m))
        if t == 1:
            squares = (z_all[0] + z_all[2]) + (z_all[4] + z_all[6])
            zz_own[...] = squares
            zz_all[k] = squares
            send(zz_own, zz_all.at[k], zz_ss.at[0], zz_rs.at[0], partner)
        for g in range(2):
            source = w_all if t == 1 else q_all
            each = [source[m].astype(jnp.float32) for m in range(g, 8, 2)]
            both_g = (each[0] + each[1]) + (each[2] + each[3])
            u_all[t, k, g] = both_g
            u_own[t, g] = both_g
        send(u_own.at[t], u_all.at[t, k], u_ss.at[t], u_rs.at[t], partner)

    def query_in(t):
        if t == 1:
            wait_arrival(zz_all.at[other], zz_ss.at[0], zz_rs.at[0], partner)
        wait_arrival(u_all.at[t, other], u_ss.at[t], u_rs.at[t], partner)

    def attend(t, g, scale):
        query = u_all[t, 0, g] + u_all[t, 1, g]
        if scale is not None:
            query = query * scale
        query = query.astype(jnp.bfloat16).astype(jnp.float32)
        spread = jnp.concatenate(
            [jnp.where(col_head == h, query, 0.0) for h in range(4)], axis=0
        ).astype(jnp.bfloat16)
        scores = lax.dot_general(
            spread, kv[2 * g], (((1,), (1,)), ((), ())), preferred_element_type=jnp.float32
        ) * 0.125
        top = jnp.max(scores, axis=-1, keepdims=True)
        expo = jnp.exp(scores - top)
        total = jnp.sum(expo, axis=-1, keepdims=True)
        mixed = jnp.dot(expo.astype(jnp.bfloat16), kv[2 * g + 1], preferred_element_type=jnp.float32)
        ctx = jnp.zeros((BEAMS, 256), jnp.float32)
        stats = jnp.zeros((8, 128), jnp.float32)
        for h in range(4):
            ctx += jnp.where(col_head == h, mixed[16 * h:16 * h + 16], 0.0)
            for half in range(2):
                at = 16 * h + 8 * half
                stats = jnp.where(lane == 8 * half + h, top[at:at + 8], stats)
                stats = jnp.where(lane == 8 * half + 4 + h, total[at:at + 8], stats)
        return ctx.astype(jnp.bfloat16), stats

    def project(g):
        @pl.loop(0, 2)
        def _(i):
            at = 2 * g + i
            kv[at] = jnp.dot(nbuf[...], wbuf[at], preferred_element_type=jnp.float32).astype(jnp.bfloat16)

    z_on(0, 0)
    z_on(0, 1)
    e_near(0)
    e_far(0)
    e_near(1)
    e_far(1)
    x_out(0, 0)
    x_out(0, 1)
    send(shard_both(k), shard_both(k), wc_ss.at[0, 0], wc_rs.at[0, 0], partner)

    for copy in loads:
        copy.wait()
    for i in range(BEAMS):
        picked[pl.ds(i, 1), :] = first[pl.ds(parents[0, i], 1), :]
    start = picked[...] + tokens[0].astype(jnp.float32)
    pre[...] = start
    mean = jnp.sum(start * start, axis=-1, keepdims=True) * (1.0 / 4096.0)
    picked[...] = start * lax.rsqrt(mean + 1e-06) * gain[...]
    q_own[...] = jnp.dot(picked[:, feats].astype(jnp.bfloat16), wq[...], preferred_element_type=jnp.float32)
    q_all[n] = q_own[...]

    z_step(1, 0)
    z_step(2, 0)
    z_step(1, 1)
    z_step(2, 1)
    x_relay(0)
    e_step(1, 0)
    e_step(1, 1)
    z_step(3, 0)
    z_step(4, 0)
    z_step(3, 1)
    z_step(4, 1)
    e_step(2, 0)
    e_step(2, 1)
    y_relay(1)
    y_relay(2)
    x_relay(1)
    z_step(5, 0)
    z_step(6, 0)
    z_step(5, 1)
    z_step(6, 1)
    x_last(0)
    y_relay(3)
    y_relay(4)
    y_cross(1)
    y_cross(2)
    x_relay(2)
    x_last(1)
    e_step(3, 0)
    e_step(3, 1)
    z_step(7, 0)
    z_step(7, 1)
    query_out(0)
    y_last(1)
    y_last(2)
    y_relay(5)
    y_relay(6)
    y_cross(3)
    y_cross(4)
    x_relay(3)
    y_last(3)
    y_last(4)
    x_last(2)
    y_relay(7)
    y_cross(5)
    y_cross(6)
    y_last(5)
    y_last(6)
    x_last(3)

    @pl.loop(0, 8)
    def _(i):
        at = pl.ds(pl.multiple_of(i * 64, 64), 64)
        acc = jnp.zeros((64, 128), jnp.float32)
        for f in range(HEAD):
            block = ebuf[f, at, :].astype(jnp.float32)
            block = block * block
            acc += block[:, :128] + block[:, 128:]
        scale = lax.rsqrt(jnp.sum(acc, axis=-1, keepdims=True) * (1.0 / 4096.0) + 1e-06)
        for f in range(HEAD):
            cols = slice(256 * f, 256 * f + 256)
            block = ebuf[f, at, :].astype(jnp.float32) * scale * enc_gain[:, cols]
            nbuf[at, cols] = block.astype(jnp.bfloat16)

    y_cross(7)
    y_last(7)
    query_swap(0)

    for q in (1, 2, 5, 6):
        for j in range(4):
            wait_arrival(both(q, j, other), wc_ss.at[q, j], wc_rs.at[q, j], partner)
    project(1 - r)
    wait_arrival(shard_both(other), wc_ss.at[0, 0], wc_rs.at[0, 0], partner)
    for q in (3, 4, 7):
        for j in range(4):
            wait_arrival(both(q, j, other), wc_ss.at[q, j], wc_rs.at[q, j], partner)
    project(r)

    for t in range(STEPS):
        scale = None
        if t == 1:
            for j in range(4):
                part[:, 128 * j:128 * j + 128] = l_all[:, j, :]
            part[...] = part[...] + pre[:, feats]
            for i in range(BEAMS):
                local_rows[pl.ds(i, 1), :] = part[pl.ds(parents[1, i], 1), :]
            rows = local_rows[...] + tokens[1, :, feats].astype(jnp.float32)
            squares = jnp.sum(rows * rows, axis=-1, keepdims=True)
            z_own[...] = fold(
                jnp.where(lane == 0, squares[:8], jnp.where(lane == 1, squares[8:], 0.0))
            )
            z_all[n] = z_own[...]
            scaled = rows * gain[:, feats]
            high = scaled.astype(jnp.bfloat16)
            low = (scaled - high.astype(jnp.float32)).astype(jnp.bfloat16)
            partial = jnp.dot(high, wq[...], preferred_element_type=jnp.float32) + jnp.dot(
                low, wq[...], preferred_element_type=jnp.float32
            )
            w_own[...] = partial.astype(jnp.bfloat16)
            w_all[n] = w_own[...]
            query_out(1)
            query_swap(1)
        query_in(t)
        if t == 1:
            table = lax.rsqrt(unfold(zz_all[0] + zz_all[1]) * (1.0 / 4096.0) + 1e-06)
            scale = jnp.concatenate([table[:, :1], table[:, 1:2]], axis=0)
        for slot, g, order in ((1, r, (3, 1, 5)), (0, 1 - r, (2, 4, 0, 6))):
            ctx, stats = attend(t, g, scale)
            c_own[t, slot] = ctx
            t_own[t, slot] = fold(stats)
            for i in order:
                m = ring_peers[i]
                send(t_own.at[t, slot], t_all.at[t, n], t_ss.at[t, i], t_rs.at[t, n], ring(m))
                send(c_own.at[t, slot], c_all.at[t, n], c_ss.at[t, i], c_rs.at[t, n], ring(m))
        c_all[t, n] = c_own[t, 1]
        t_all[t, n] = t_own[t, 1]
        if t == 1:
            for i, p in enumerate(seq_peers):
                wait_arrival(f_all.at[0, p], f_ss.at[0, i], f_rs.at[0, p], {"seq": p})
            for i, p in enumerate(head_peers):
                send(f_all.at[0], g_all.at[0, c], g_ss.at[0, i], g_rs.at[0, c], {"head": p})
            g_all[0, c] = f_all[0]
            for i, p in enumerate(head_peers):
                wait_arrival(g_all.at[0, p], g_ss.at[0, i], g_rs.at[0, p], {"head": p})
            for i in range(8):
                for j in range(4):
                    cols = slice(512 * i + 128 * j, 512 * i + 128 * j + 128)
                    one_col = g_all[0, :, i, j, :]
                    out_first[:, cols] = one_col
                    full[:, cols] = pre[:, cols] + one_col
            for i in range(BEAMS):
                picked[pl.ds(i, 1), :] = full[pl.ds(parents[1, i], 1), :]
            out_pre[...] = picked[...] + tokens[1].astype(jnp.float32)
            stores = [
                pltpu.make_async_copy(out_pre, pre_out, out_sem.at[0]),
                pltpu.make_async_copy(out_first, first_out, out_sem.at[1]),
            ]
            for copy in stores:
                copy.start()
        for i, m in enumerate(ring_peers):
            wait_arrival(t_all.at[t, m], t_ss.at[t, i], t_rs.at[t, m], ring(m))
            wait_arrival(c_all.at[t, m], c_ss.at[t, i], c_rs.at[t, m], ring(m))
        peak, sums, joined = merge(
            [unfold(t_all[t, i]) for i in range(8)], [c_all[t, i].astype(jnp.float32) for i in range(8)]
        )
        stats = jnp.where(is_top, peak, pltpu.roll(sums, 4, 1))
        v_own[t] = joined
        m_own[t] = stats
        v_all[t, k] = joined
        m_all[t, k] = stats
        send(m_own.at[t], m_all.at[t, k], m_ss.at[t], m_rs.at[t], partner)
        send(v_own.at[t], v_all.at[t, k], v_ss.at[t], v_rs.at[t], partner)
        wait_arrival(m_all.at[t, other], m_ss.at[t], m_rs.at[t], partner)
        wait_arrival(v_all.at[t, other], v_ss.at[t], v_rs.at[t], partner)
        peak, sums, joined = merge([m_all[t, 0], m_all[t, 1]], [v_all[t, 0], v_all[t, 1]])
        context = (joined / spread_rows(sums)).astype(jnp.bfloat16)
        partial = jnp.dot(context, wo[...], preferred_element_type=jnp.float32)
        for j in range(4):
            p_own[t, :, j, :] = partial[:, 128 * j:128 * j + 128]
        p_all[t, c] = p_own[t, c]
        for i, p in enumerate(head_peers):
            send(p_own.at[t, p], p_all.at[t, c], p_ss.at[t, i], p_rs.at[t, c], {"head": p})
        for i, p in enumerate(head_peers):
            wait_arrival(p_all.at[t, p], p_ss.at[t, i], p_rs.at[t, p], {"head": p})
        row = p_all[t, 0]
        for i in range(1, HEAD):
            row += p_all[t, i]
        f_own[t] = row
        f_all[t, s] = row
        if t == 0:
            for i, p in enumerate(head_peers):
                send(f_own.at[t], l_all.at[c], l_ss.at[i], l_rs.at[c], {"head": p})
            l_all[c] = row
        for i, p in enumerate(seq_peers):
            send(f_own.at[t], f_all.at[t, s], f_ss.at[t, i], f_rs.at[t, s], {"seq": p})
        if t == 0:
            for i, p in enumerate(head_peers):
                wait_arrival(l_all.at[p], l_ss.at[i], l_rs.at[p], {"head": p})
    z_hi = lax.div(s, 2)
    slices = [lax.rem(z_hi + i, 4) for i in (0, 1, 3, 2)]
    for i, z_from in enumerate(slices):
        for core in (0, 1):
            if i == 0:
                continue
            p = 2 * z_from + core
            wait_arrival(f_all.at[1, p], f_ss.at[1, 0], f_rs.at[1, p], partner)
        if i == 0:
            wait_arrival(f_all.at[1, s + 1 - 2 * k], f_ss.at[1, 0], f_rs.at[1, s + 1 - 2 * k], partner)
        two = pl.ds(2 * z_from, 2)
        for h, p in enumerate(head_peers):
            send(f_all.at[1, two], g_all.at[1, c, two], e_ss.at[i, h], e_rs.at[i, c], {"head": p})
    g_all[1, c] = f_all[1]
    for i, z_from in enumerate(slices):
        two = pl.ds(2 * z_from, 2)
        for h, p in enumerate(head_peers):
            wait_arrival(g_all.at[1, p, two], e_ss.at[i, h], e_rs.at[i, p], {"head": p})
    for i in range(8):
        for j in range(4):
            cols = slice(512 * i + 128 * j, 512 * i + 128 * j + 128)
            one_col = g_all[1, :, i, j, :]
            out_second[:, cols] = one_col
    stores.append(pltpu.make_async_copy(out_second, second_out, out_sem.at[2]))
    stores[2].start()
    for copy in sent:
        copy.wait_send()
    for copy in stores:
        copy.wait()


def on_device(
    enc_out, enc_gain, key_weight, value_weight, query_weight, out_weight,
    dec_gain, beam_state, parents, token_embed,
):
    anywhere = pl.BlockSpec(memory_space=pl.ANY)
    f32, bf16 = jnp.float32, jnp.bfloat16
    dma = pltpu.SemaphoreType.DMA
    rows = jax.ShapeDtypeStruct((BEAMS, 4096), f32)

    def pair(*shape):
        return [dma(shape), dma(shape)]

    before, once, twice = pl.pallas_call(
        kernel,
        out_shape=(rows, rows, rows),
        in_specs=[anywhere] * 8 + [pl.BlockSpec(memory_space=pltpu.SMEM), anywhere],
        out_specs=(anywhere, anywhere, anywhere),
        scratch_shapes=[
            pltpu.VMEM((1, 4096), f32),
            pltpu.VMEM((512, 256), bf16),
            pltpu.VMEM((256, 512), bf16),
            pltpu.VMEM((1, 4096), f32),
            pltpu.VMEM((BEAMS, 4096), f32),
            pltpu.VMEM((STEPS, BEAMS, 4096), bf16),
            pltpu.VMEM((BEAMS, 4096), f32),
            pltpu.VMEM((BEAMS, 4096), f32),
            pltpu.VMEM((BEAMS, 4096), f32),
            pltpu.VMEM((HEAD, 512, 256), bf16),
            pltpu.VMEM((512, 4096), bf16),
            pltpu.VMEM((4, 4096, 256), bf16),
            pltpu.VMEM((4, 512, 256), bf16),
            pltpu.VMEM((BEAMS, 4096), f32),
            pltpu.VMEM((BEAMS, 512), f32),
            pltpu.VMEM((BEAMS, 4096), f32),
            pltpu.VMEM((BEAMS, 512), f32),
            pltpu.VMEM((BEAMS, 4096), f32),
            pltpu.VMEM((BEAMS, 256), f32),
            pltpu.VMEM((8, BEAMS, 256), f32),
            pltpu.VMEM((BEAMS, 256), bf16),
            pltpu.VMEM((8, BEAMS, 256), bf16),
            pltpu.VMEM((STEPS, 2, BEAMS, 256), f32),
            pltpu.VMEM((STEPS, 2, 2, BEAMS, 256), f32),
            pltpu.VMEM((1, 128), f32),
            pltpu.VMEM((8, 1, 128), f32),
            pltpu.VMEM((1, 128), f32),
            pltpu.VMEM((2, 1, 128), f32),
            pltpu.VMEM((STEPS, 2, BEAMS, 256), bf16),
            pltpu.VMEM((STEPS, 8, BEAMS, 256), bf16),
            pltpu.VMEM((STEPS, 2, 1, 128), f32),
            pltpu.VMEM((STEPS, 8, 1, 128), f32),
            pltpu.VMEM((STEPS, 8, 128), f32),
            pltpu.VMEM((STEPS, 2, 8, 128), f32),
            pltpu.VMEM((STEPS, BEAMS, 256), f32),
            pltpu.VMEM((STEPS, 2, BEAMS, 256), f32),
            pltpu.VMEM((STEPS, BEAMS, 4, 128), f32),
            pltpu.VMEM((STEPS, HEAD, 4, 128), f32),
            pltpu.VMEM((STEPS, 4, 128), f32),
            pltpu.VMEM((STEPS, SEQ, 4, 128), f32),
            pltpu.VMEM((BEAMS, 4, 128), f32),
            pltpu.VMEM((STEPS, BEAMS, 8, 4, 128), f32),
            dma((3,)), dma((6,)), dma((3,)),
            *pair(8, 2), *pair(8, 2, 2), *pair(8, 2), *pair(8, 4), *pair(3, 2), *pair(4, 2, 2), *pair(4, 2),
            *pair(STEPS, 8), *pair(STEPS), *pair(8), *pair(1), *pair(STEPS, 8), *pair(STEPS, 8),
            *pair(STEPS), *pair(STEPS), *pair(STEPS, HEAD), *pair(STEPS, SEQ), *pair(HEAD), *pair(STEPS, HEAD), *pair(4, HEAD),
        ],
        compiler_params=pltpu.CompilerParams(collective_id=1, has_side_effects=True),
        name="beam_decode",
    )(
        enc_out, enc_gain.reshape(1, 4096), key_weight, value_weight, query_weight, out_weight,
        dec_gain.reshape(1, 4096), beam_state, parents, token_embed,
    )
    return before + twice, once + twice


def solution(mesh):
    placed = (
        P(("src", "seq"), "head"),
        P(),
        P("seq", "head"),
        P("seq", "head"),
        P("seq", "head"),
        P("head", "seq"),
        P(),
        P("src", None),
        P("src", None),
        P("src", None, None),
    )
    return jax.shard_map(
        on_device,
        mesh=mesh,
        in_specs=placed,
        out_specs=(P("src", None), P("src", None)),
        check_vma=False,
    )
```
